256 devices in a mesh: samp: 32 (over z_hi, y, x), feat: 8 (over z_lo, core).
Axes of the slice: x: 4, y: 4, z: 8 (z_hi: 2, z_lo: 4; z = z_hi * 4 + z_lo), core: 2. Of those that a mesh axis runs over, the one named last changes fastest.
Arguments:
- counters: bfloat16 [32768, 512], P('samp'), may hold values from -6 to 6
- frequencies: bfloat16 [512, 4096], P(None, 'feat'), may hold values from -0.25 to 0.25
- phases: bfloat16 [1, 4096], P(None, 'feat'), may hold values from -3.140625 to 3.140625
- targets: bfloat16 [32768, 64], P('samp'), may hold values from -6 to 6
Outputs:
- solution: float32 [4096, 64], P('samp')
- residual: float32 [4096, 64], P('samp')
- gram: float32 [4096, 4096], P('samp', 'feat')
The draws below stay inside these ranges and needn't reach their ends.
All inputs are finite; a program needn't handle non-finite values.
Results may differ from the reference program's by a relative error of at most 0.0035.
Values may be sent and summed in bfloat16 or wider, within the bound.
A program may use at most 64 MiB of HBM per device.

```python
import math
import jax
import jax.numpy as jnp
from jax import lax

COUNTERS = 512
FEATURES = 4096
TARGETS = 64
ROWS_DEV = 1024
ITERS = 2
TOTAL = 32768


def block_levels(own_key, dims, cuts, smallest, largest):
    def one(position, shards_of):
        heights = jax.random.uniform(jax.random.fold_in(jax.random.fold_in(own_key, 6), position), (shards_of,), jnp.float32, smallest / len(cuts), largest / len(cuts))
        return jnp.repeat(jnp.exp(heights), dims[position] // shards_of).reshape((-1,) + (1,) * (len(dims) - position - 1))

    level = one(*cuts[0])
    for cut in cuts[1:]:
        level = level * one(*cut)
    return level


def scatter_about(rng, dims, width, reach, split=(), held_as=jnp.bfloat16):
    values = width * jax.random.normal(rng, dims, jnp.float32)
    if split:
        values = values * block_levels(rng, dims, split, -0.22, 0.18)
    return jnp.clip(values, -reach, reach).astype(held_as)


def setup_inputs(seed: int = 0) -> dict:
    streams_of = jax.random.split(jax.random.key(seed), 5)
    counters = scatter_about(streams_of[0], (TOTAL, COUNTERS), 1.0, 6.0, ((0, 32),))
    frequencies = scatter_about(streams_of[1], (COUNTERS, FEATURES), COUNTERS ** -0.5, 0.25, ((1, 8),))
    phases = jnp.clip(jax.random.uniform(streams_of[2], (1, FEATURES), jnp.float32, -3.140625, 3.140625), -3.140625, 3.140625).astype(jnp.bfloat16)
    targets = scatter_about(streams_of[3], (TOTAL, TARGETS), 1.0, 6.0, ((0, 32),))
    return {"counters": counters, "frequencies": frequencies, "phases": phases, "targets": targets}


RIDGE = 0.05

def make_features(counters, frequencies, phases):
    mixed = jnp.dot(counters, frequencies, preferred_element_type=jnp.float32)
    return jnp.cos(mixed + phases.astype(jnp.float32)).astype(jnp.bfloat16)

def reference(counters, frequencies, phases, targets):
    samples = counters.shape[0]
    blocks = samples // ROWS_DEV
    inputs = counters.reshape(blocks, ROWS_DEV, COUNTERS)
    outputs = targets.reshape(blocks, ROWS_DEV, TARGETS)
    inner = (((0,), (0,)), ((), ()))

    def accumulate(carry, pair):
        gram, right = carry
        zeta = make_features(pair[0], frequencies, phases)
        gram = gram + lax.dot_general(zeta, zeta, inner, preferred_element_type=jnp.float32)
        right = right + lax.dot_general(zeta, pair[1], inner, preferred_element_type=jnp.float32)
        return ((gram, right), None)
    start_vals = (jnp.zeros((FEATURES, FEATURES), jnp.float32), jnp.zeros((FEATURES, TARGETS), jnp.float32))
    (gram, right), _ = lax.scan(accumulate, start_vals, (inputs, outputs))
    gram = gram / samples
    right = right / math.sqrt(samples)

    def operate(vector):
        return jnp.dot(gram, vector, precision=lax.Precision.HIGHEST) + RIDGE * vector
    solution = jnp.zeros_like(right)
    residual = right
    direction = right
    norm_now = lax.optimization_barrier(jnp.sum(residual * residual, axis=0))
    for iteration in range(ITERS):
        image = operate(direction)
        step_size = norm_now / lax.optimization_barrier(jnp.sum(direction * image, axis=0))
        solution = solution + step_size * direction
        residual = residual - step_size * image
        norm_next = lax.optimization_barrier(jnp.sum(residual * residual, axis=0))
        direction = residual + norm_next / norm_now * direction
        norm_now = norm_next
    return (solution, residual, gram)
```

```python
import math

import jax
import jax.numpy as jnp
from jax import lax
from jax.experimental import pallas as pl
from jax.experimental.pallas import tpu as pltpu
from jax.sharding import PartitionSpec as P

RIDGE = 0.05
ROWS, DEPTH, WIDTH, TARGETS, BLOCK = 1024, 512, 512, 64, 128
TOTAL = 32768
STEP = 512
MESH = pl.DeviceIdType.MESH
SINE = (4.442883014678955, -7.308241367340088, 3.6062889099121094, -0.8457635641098022, 0.10920573770999908)
HIGHEST = lax.Precision.HIGHEST
F32 = jnp.float32


def cosine(angle):
    turns = angle * (0.5 / math.pi)
    f = turns - jnp.round(turns)
    square = f * f
    poly = SINE[-1]
    for coefficient in SINE[-2::-1]:
        poly = poly * square + coefficient
    root = poly * f
    return (1.0 - root * root).astype(jnp.bfloat16)


def remote(src, dst, send_sem, recv_sem, device):
    return pltpu.make_async_remote_copy(
        src_ref=src, dst_ref=dst, send_sem=send_sem, recv_sem=recv_sem, device_id=device, device_id_type=MESH
    )


def greet(peers):
    barrier = pltpu.get_barrier_semaphore()
    for peer in peers:
        pl.semaphore_signal(barrier, inc=1, device_id=peer, device_id_type=MESH)
    pl.semaphore_wait(barrier, len(peers))


def gather_kernel(cnt, tgt, frq, cg, tg, fr, ssem, rsem, fsend, frecv, lsem):
    s, j = lax.axis_index("samp"), lax.axis_index("feat")
    x, c, zl, zh = lax.rem(s, 4), lax.rem(j, 2), lax.div(j, 2), lax.div(s, 16)
    z = zh * 4 + zl
    right = (s - x + lax.rem(x + 1, 4), j)
    left = (s - x + lax.rem(x + 3, 4), j)
    sibling = (s, j + 1 - 2 * c)

    def along_z(dz, core):
        other = lax.rem(z + dz + 8, 8)
        return (lax.div(other, 4) * 16 + lax.rem(s, 16), lax.rem(other, 4) * 2 + core)

    far = 2 - 4 * c
    greet(
        [right, left, sibling]
        + [along_z(dz, core) for dz in (1, -1) for core in (0, 1)]
        + [along_z(far, 0), along_z(far, 1), along_z(-far, c)]
    )

    half = STEP * c
    a_rows, b_rows = pl.ds(pl.multiple_of(half, 256), 256), pl.ds(pl.multiple_of(half + 256, 256), 256)
    a_cols = pl.ds(pl.multiple_of(half, 256), 256)
    b_cols = pl.ds(pl.multiple_of(half + 256, 256), 256)

    def pair(i, src_c, src_t, slot, part, device):
        rows, cols = (a_rows, a_cols) if part == 0 else (b_rows, b_cols)
        return [
            remote(src_c.at[rows], cg.at[slot, rows], ssem.at[2 * i], rsem.at[2 * i], device),
            remote(src_t.at[:, cols], tg.at[slot, :, cols], ssem.at[2 * i + 1], rsem.at[2 * i + 1], device),
        ]

    def twin(i, slot, part):
        other = STEP - half
        rows = pl.ds(pl.multiple_of(other + 256 * part, 256), 256)
        cols = pl.ds(pl.multiple_of(other + 256 * part, 256), 256)
        return [
            remote(cg.at[slot, rows], cg.at[slot, rows], ssem.at[2 * i], rsem.at[2 * i], sibling),
            remote(tg.at[slot, :, cols], tg.at[slot, :, cols], ssem.at[2 * i + 1], rsem.at[2 * i + 1], sibling),
        ]

    to_right = [pair(0, cnt, tgt, 1, 0, right), pair(1, cnt, tgt, 1, 1, right)]
    to_left = [pair(2, cnt, tgt, 2, 0, left), pair(3, cnt, tgt, 2, 1, left)]
    on_right = pair(4, cg.at[1], tg.at[1], 3, 0, right)
    on_left = pair(5, cg.at[2], tg.at[2], 3, 1, left)
    across = {
        (slot, part): pair(6 + 2 * (slot - 1) + part, cg.at[slot], tg.at[slot], slot, part, sibling)
        for slot in (1, 2, 3)
        for part in (0, 1)
    }

    def go(copies):
        for copy in copies:
            copy.start()

    def got(copies):
        for copy in copies:
            copy.wait_recv()

    go(to_right[0])
    go(to_left[1])
    quarter = pl.ds(pl.multiple_of(BLOCK * x, BLOCK), BLOCK)
    mine = pl.ds(pl.multiple_of(BLOCK * j, BLOCK), BLOCK)
    spread = []
    for i, (dz, core) in enumerate([(1, 0), (1, 1), (-1, 0), (-1, 1), (far, 0), (far, 1)]):
        spread.append(remote(frq.at[quarter], fr.at[mine], fsend.at[i], frecv.at[2 * (i // 2) + c], along_z(dz, core)))
    spread.append(remote(frq.at[quarter], fr.at[mine], fsend.at[6], frecv.at[6], sibling))
    go(spread)
    go(to_right[1])
    go(to_left[0])
    local = [
        pltpu.make_async_copy(cnt, cg.at[0], lsem.at[0]),
        pltpu.make_async_copy(tgt, tg.at[0], lsem.at[1]),
        pltpu.make_async_copy(frq.at[quarter], fr.at[mine], lsem.at[2]),
    ]
    go(local)
    got(to_right[0])
    go(on_right)
    go(across[1, 0])
    got(to_left[1])
    go(on_left)
    go(across[2, 1])
    got(to_right[1])
    go(across[1, 1])
    got(to_left[0])
    go(across[2, 0])
    got(on_right)
    go(across[3, 0])
    got(on_left)
    go(across[3, 1])
    for (slot, part), copies in across.items():
        got(twin(6 + 2 * (slot - 1) + part, slot, part))
    for i, (dz, core) in enumerate([(-1, 0), (-1, 1), (1, 0), (1, 1), (-2, 0), (2, 1)]):
        source = along_z(dz, core)
        rows = pl.ds(pl.multiple_of(BLOCK * source[1], BLOCK), BLOCK)
        remote(frq.at[quarter], fr.at[rows], fsend.at[i], frecv.at[2 * (i // 2) + core], source).wait_recv()
    rows = pl.ds(pl.multiple_of(BLOCK * sibling[1], BLOCK), BLOCK)
    remote(frq.at[quarter], fr.at[rows], fsend.at[6], frecv.at[6], sibling).wait_recv()
    for copy in local:
        copy.wait()
    sent = to_right[0] + to_right[1] + to_left[0] + to_left[1] + on_right + on_left + spread
    for copies in across.values():
        sent = sent + copies
    for copy in sent:
        copy.wait_send()


def gather(counters, targets, frequencies):
    bf16 = jnp.bfloat16
    hbm = pl.BlockSpec(memory_space=pl.ANY)
    return pl.pallas_call(
        gather_kernel,
        out_shape=(
            jax.ShapeDtypeStruct((4, ROWS, DEPTH), bf16),
            jax.ShapeDtypeStruct((4, TARGETS, ROWS), bf16),
            jax.ShapeDtypeStruct((8 * BLOCK, DEPTH + 128), bf16),
        ),
        in_specs=[hbm] * 3,
        out_specs=(hbm,) * 3,
        scratch_shapes=[
            pltpu.SemaphoreType.DMA((24,)),
            pltpu.SemaphoreType.DMA((24,)),
            pltpu.SemaphoreType.DMA((7,)),
            pltpu.SemaphoreType.DMA((7,)),
            pltpu.SemaphoreType.DMA((3,)),
        ],
        compiler_params=pltpu.CompilerParams(collective_id=0, has_side_effects=True, vmem_limit_bytes=4 << 20),
        name="gather",
    )(counters, targets, frequencies)


def build_kernel(cnt, tgt, frow, fcol, phase, part, rhs, zrow, gram, right):
    step = pl.program_id(0)
    j = lax.axis_index("feat")

    @pl.when(step == 0)
    def _():
        gram[...] = jnp.zeros_like(gram)
        right[...] = jnp.zeros_like(right)

    nt = (((1,), (1,)), ((), ()))
    rows = cnt[...]
    zcol = cosine(jnp.dot(rows, fcol[...], preferred_element_type=F32) + phase[...].astype(F32))
    mixed = lax.dot_general(frow[:, :DEPTH], rows, nt, preferred_element_type=F32)
    zrow[...] = cosine(mixed + frow[:, DEPTH : DEPTH + 1].astype(F32))
    gram[...] += jnp.dot(zrow[...], zcol, preferred_element_type=F32)
    own = zrow[pl.ds(pl.multiple_of(BLOCK * j, BLOCK), BLOCK), :]
    right[...] += lax.dot_general(tgt[0], own, nt, preferred_element_type=F32)

    @pl.when(step == pl.num_programs(0) - 1)
    def _():
        for block in range(8):
            part[block % 4, block // 4] = gram[block * BLOCK : (block + 1) * BLOCK, :]
        rhs[...] = right[...]


def build(counters, targets, frow, fcol, phases):
    steps = 4 * ROWS // STEP
    per = ROWS // STEP
    whole = lambda shape: pl.BlockSpec(shape, lambda i: (0,) * len(shape))
    return pl.pallas_call(
        build_kernel,
        out_shape=(
            jax.ShapeDtypeStruct((4, 2, BLOCK, WIDTH), F32),
            jax.ShapeDtypeStruct((TARGETS, BLOCK), F32),
        ),
        grid=(steps,),
        in_specs=[
            pl.BlockSpec((STEP, DEPTH), lambda i: (i, 0)),
            pl.BlockSpec((1, TARGETS, STEP), lambda i: (i // per, 0, i % per)),
            whole((8 * BLOCK, DEPTH + 128)),
            whole((DEPTH, WIDTH)),
            whole((1, WIDTH)),
        ],
        out_specs=(whole((4, 2, BLOCK, WIDTH)), whole((TARGETS, BLOCK))),
        scratch_shapes=[
            pltpu.VMEM((8 * BLOCK, STEP), jnp.bfloat16),
            pltpu.VMEM((8 * BLOCK, WIDTH), F32),
            pltpu.VMEM((TARGETS, BLOCK), F32),
        ],
        compiler_params=pltpu.CompilerParams(vmem_limit_bytes=40 << 20),
        name="build",
    )(counters.reshape(4 * ROWS, DEPTH), targets, frow, fcol, phases)


def solve_kernel(
    part, rhs, sol, res, gram,
    ybuf, zsend, zrecv, rh, vj, pout, fb, stat, xb, tot, db, keep, fin,
    ssem, hsem, ysem, zsem, bsem, asem, fsem, xsem, dsem, esem,
):
    s, j = lax.axis_index("samp"), lax.axis_index("feat")
    x, b = lax.rem(s, 4), lax.div(s, 4)
    y, zh = lax.rem(b, 4), lax.div(b, 4)
    diag = b == j
    xmates = [(b * 4 + lax.rem(x + d, 4), j) for d in (1, 2, 3)]
    bothers = [lax.rem(b + e, 8) for e in range(1, 8)]
    bmates = [(o * 4 + x, j) for o in bothers]
    fothers = [lax.rem(j + e, 8) for e in range(1, 8)]
    fmates = [(s, o) for o in fothers]
    dmates = [(o * 4 + x, o) for o in bothers]
    barrier = pltpu.get_barrier_semaphore()
    for peer in xmates + bmates + fmates:
        pl.semaphore_signal(barrier, inc=1, device_id=peer, device_id_type=MESH)

    @pl.when(diag)
    def _():
        for peer in dmates:
            pl.semaphore_signal(barrier, inc=1, device_id=peer, device_id_type=MESH)

    pl.semaphore_wait(barrier, jnp.where(diag, 24, 17))

    count = [0]
    sent, sent_diag = [], []

    def copy(src, dst, recv_sem, device):
        made = remote(src, dst, ssem.at[count[0]], recv_sem, device)
        count[0] += 1
        return made

    def wait(ref, sem):
        remote(ref, ref, ssem.at[0], sem, xmates[0]).wait_recv()

    send_rhs = copy(rhs, rh.at[b], hsem.at[b], (j * 4 + x, j))

    @pl.when(jnp.logical_not(diag))
    def _():
        send_rhs.start()

    for d in (1, 2, 3):
        to = lax.rem(y + d, 4)
        made = copy(part.at[to], ybuf.at[d - 1], ysem.at[d - 1], ((zh * 4 + to) * 4 + x, j))
        made.start()
        sent.append(made)
    for d in (1, 2, 3):
        wait(ybuf.at[d - 1], ysem.at[d - 1])

    def over_y(which):
        total = part[y, which]
        for d in range(3):
            total = total + ybuf[d, which]
        return total

    zsend[...] = over_y(1 - zh)
    send_z = copy(zsend, zrecv, zsem, (((1 - zh) * 4 + y) * 4 + x, j))
    send_z.start()
    sent.append(send_z)
    gram[...] = over_y(zh)

    own = pl.ds(pl.multiple_of(BLOCK * x, BLOCK), BLOCK)

    @pl.when(diag)
    def _():
        total = rhs[...]
        for o in bothers:
            wait(rh.at[o], hsem.at[o])
            total = total + rh[o]
        first = total * (1.0 / math.sqrt(TOTAL))
        keep[0] = first
        vj[0, :, own] = first

    def distribute(it):
        sends = [copy(vj.at[it, :, own], vj.at[it, :, own], bsem.at[it], peer) for peer in bmates]
        sent_diag.extend(sends)

        @pl.when(diag)
        def _():
            for made in sends:
                made.start()

        @pl.when(jnp.logical_not(diag))
        def _():
            wait(vj.at[it, :, own], bsem.at[it])

        for d in (1, 2, 3):
            made = copy(vj.at[it, :, own], vj.at[it, :, own], asem.at[3 * it + d - 1], xmates[d - 1])
            made.start()
            sent.append(made)

    def collect(it):
        for d in (1, 2, 3):
            slot = pl.ds(pl.multiple_of(BLOCK * lax.rem(x + 4 - d, 4), BLOCK), BLOCK)
            wait(vj.at[it, :, slot], asem.at[3 * it + d - 1])

    sent_off = [send_rhs]

    def multiply(it):
        pout[it] = lax.dot_general(
            vj[it], gram[...], (((1,), (1,)), ((), ())), precision=HIGHEST, preferred_element_type=F32
        )
        made = copy(pout.at[it], fb.at[it, j], fsem.at[8 * it + j], (s, b))
        sent_off.append(made)

        @pl.when(jnp.logical_not(diag))
        def _():
            made.start()

    def image(it, vector):
        total = pout[it] + RIDGE * vector
        for o in fothers:
            wait(fb.at[it, o], fsem.at[8 * it + o])
            total = total + fb[it, o]
        return total

    def columns(index):
        return jnp.sum(tot[index], axis=1, keepdims=True)

    planes = [pl.ds(0, 2), pl.ds(2, 1), pl.ds(3, 1)]
    x_sends = [
        [copy(stat.at[p], xb.at[d, p], xsem.at[3 * k + d], xmates[d]) for d in range(3)] for k, p in enumerate(planes)
    ]
    d_sends = [
        [copy(tot.at[p], db.at[e, p], dsem.at[7 * k + e], dmates[e]) for e in range(7)] for k, p in enumerate(planes)
    ]
    for group in x_sends + d_sends:
        sent_diag.extend(group)

    def sum_start(k):
        for made in x_sends[k]:
            made.start()

    def sum_finish(k):
        p = planes[k]
        total = stat[p]
        for d in range(3):
            wait(xb.at[d, p], xsem.at[3 * k + d])
            total = total + xb[d, p]
        tot[p] = total
        for made in d_sends[k]:
            made.start()
        for e in range(7):
            wait(db.at[e, p], dsem.at[7 * k + e])
            total = total + db[e, p]
        for made in d_sends[k]:
            made.wait_send()
        tot[p] = total

    distribute(0)
    collect(0)
    wait(zrecv, zsem)
    gram[...] = (gram[...] + zrecv[...]) * (1.0 / TOTAL)
    multiply(0)

    @pl.when(diag)
    def _():
        first = keep[0]
        w1 = image(0, first)
        keep[1] = w1
        vj[1, :, own] = w1
        stat[0] = first * first
        stat[1] = first * w1

    distribute(1)

    @pl.when(diag)
    def _():
        sum_start(0)

    collect(1)
    multiply(1)

    final = [copy(fin, fin, esem, peer) for peer in fmates]
    sent_diag.extend(final)

    @pl.when(diag)
    def _():
        sum_finish(0)
        first, w1 = keep[0], keep[1]
        rr0 = columns(0)
        a0 = rr0 / columns(1)
        r1 = first - a0 * w1
        stat[2] = r1 * r1
        sum_start(1)
        sum_finish(1)
        rr1 = columns(2)
        b0 = rr1 / rr0
        d1 = r1 + b0 * first
        w2 = image(1, w1)
        image1 = (w1 - a0 * w2) + b0 * w1
        stat[3] = d1 * image1
        sum_start(2)
        sum_finish(2)
        a1 = rr1 / columns(3)
        fin[0] = a0 * first + a1 * d1
        fin[1] = r1 - a1 * image1
        for made in final:
            made.start()

    @pl.when(jnp.logical_not(diag))
    def _():
        wait(fin, esem)

    sol[...] = fin[0]
    res[...] = fin[1]
    for made in sent:
        made.wait_send()

    waited = [made for group in d_sends for made in group]

    @pl.when(diag)
    def _():
        for made in sent_diag:
            if not any(made is other for other in waited):
                made.wait_send()

    @pl.when(jnp.logical_not(diag))
    def _():
        for made in sent_off:
            made.wait_send()


def solve(part, rhs):
    vmem = pl.BlockSpec(memory_space=pltpu.VMEM)
    dma = pltpu.SemaphoreType.DMA
    vector = (TARGETS, BLOCK)
    return pl.pallas_call(
        solve_kernel,
        out_shape=(
            jax.ShapeDtypeStruct(vector, F32),
            jax.ShapeDtypeStruct(vector, F32),
            jax.ShapeDtypeStruct((BLOCK, WIDTH), F32),
        ),
        in_specs=[vmem] * 2,
        out_specs=(vmem,) * 3,
        scratch_shapes=[
            pltpu.VMEM((3, 2, BLOCK, WIDTH), F32),
            pltpu.VMEM((BLOCK, WIDTH), F32),
            pltpu.VMEM((BLOCK, WIDTH), F32),
            pltpu.VMEM((8,) + vector, F32),
            pltpu.VMEM((2, TARGETS, WIDTH), F32),
            pltpu.VMEM((2,) + vector, F32),
            pltpu.VMEM((2, 8) + vector, F32),
            pltpu.VMEM((4,) + vector, F32),
            pltpu.VMEM((3, 4) + vector, F32),
            pltpu.VMEM((4,) + vector, F32),
            pltpu.VMEM((7, 4) + vector, F32),
            pltpu.VMEM((2,) + vector, F32),
            pltpu.VMEM((2,) + vector, F32),
            dma((72,)),
            dma((8,)),
            dma((3,)),
            dma,
            dma((2,)),
            dma((6,)),
            dma((16,)),
            dma((9,)),
            dma((21,)),
            dma,
        ],
        compiler_params=pltpu.CompilerParams(collective_id=1, has_side_effects=True, vmem_limit_bytes=24 << 20),
        name="solve",
    )(part, rhs)


def on_device(counters, frequencies, phases, targets):
    columns = jnp.concatenate([frequencies.T, jnp.broadcast_to(phases.T, (WIDTH, 128))], axis=1)
    all_counters, all_targets, rows = gather(counters, targets.T, columns)
    part, rhs = build(all_counters, all_targets, rows, frequencies, phases)
    solution, residual, gram = solve(part, rhs)
    return solution.T, residual.T, gram


def solution(mesh):
    return jax.shard_map(
        on_device,
        mesh=mesh,
        in_specs=(P("samp", None), P(None, "feat"), P(None, "feat"), P("samp", None)),
        out_specs=(P("samp", None), P("samp", None), P("samp", "feat")),
        check_vma=False,
    )
```

```python
import math

import jax
import jax.numpy as jnp
from jax import lax
from jax.experimental import pallas as pl
from jax.experimental.pallas import tpu as pltpu
from jax.sharding import PartitionSpec as P

RIDGE = 0.05
ROWS, DEPTH, WIDTH, TARGETS, BLOCK = 1024, 512, 512, 64, 128
TOTAL = 32768
STEP = 512
MESH = pl.DeviceIdType.MESH
SINE = (4.442883014678955, -7.308241367340088, 3.6062889099121094, -0.8457635641098022, 0.10920573770999908)
HIGHEST = lax.Precision.HIGHEST
F32 = jnp.float32


def cosine(angle):
    turns = angle * (0.5 / math.pi)
    f = turns - jnp.round(turns)
    square = f * f
    poly = SINE[-1]
    for coefficient in SINE[-2::-1]:
        poly = poly * square + coefficient
    root = poly * f
    return (1.0 - root * root).astype(jnp.bfloat16)


def remote(src, dst, send_sem, recv_sem, device):
    return pltpu.make_async_remote_copy(
        src_ref=src, dst_ref=dst, send_sem=send_sem, recv_sem=recv_sem, device_id=device, device_id_type=MESH
    )


def greet(peers):
    barrier = pltpu.get_barrier_semaphore()
    for peer in peers:
        pl.semaphore_signal(barrier, inc=1, device_id=peer, device_id_type=MESH)
    pl.semaphore_wait(barrier, len(peers))


def gather_kernel(cnt, tgt, frq, cg, tg, fr, ssem, rsem, fsend, frecv, lsem):
    s, j = lax.axis_index("samp"), lax.axis_index("feat")
    x, c, zl, zh = lax.rem(s, 4), lax.rem(j, 2), lax.div(j, 2), lax.div(s, 16)
    z = zh * 4 + zl
    right = (s - x + lax.rem(x + 1, 4), j)
    left = (s - x + lax.rem(x + 3, 4), j)
    sibling = (s, j + 1 - 2 * c)

    def along_z(dz, core):
        other = lax.rem(z + dz + 8, 8)
        return (lax.div(other, 4) * 16 + lax.rem(s, 16), lax.rem(other, 4) * 2 + core)

    far = 2 - 4 * c
    greet(
        [right, left, sibling]
        + [along_z(dz, core) for dz in (1, -1) for core in (0, 1)]
        + [along_z(far, 0), along_z(far, 1), along_z(-far, c)]
    )

    half = STEP * c
    a_rows, b_rows = pl.ds(pl.multiple_of(half, 256), 256), pl.ds(pl.multiple_of(half + 256, 256), 256)
    a_cols = pl.ds(pl.multiple_of(half, 256), 256)
    b_cols = pl.ds(pl.multiple_of(half + 256, 256), 256)

    def pair(i, src_c, src_t, slot, part, device):
        rows, cols = (a_rows, a_cols) if part == 0 else (b_rows, b_cols)
        return [
            remote(src_c.at[rows], cg.at[slot, rows], ssem.at[2 * i], rsem.at[2 * i], device),
            remote(src_t.at[:, cols], tg.at[slot, :, cols], ssem.at[2 * i + 1], rsem.at[2 * i + 1], device),
        ]

    def twin(i, slot, part):
        other = STEP - half
        rows = pl.ds(pl.multiple_of(other + 256 * part, 256), 256)
        cols = pl.ds(pl.multiple_of(other + 256 * part, 256), 256)
        return [
            remote(cg.at[slot, rows], cg.at[slot, rows], ssem.at[2 * i], rsem.at[2 * i], sibling),
            remote(tg.at[slot, :, cols], tg.at[slot, :, cols], ssem.at[2 * i + 1], rsem.at[2 * i + 1], sibling),
        ]

    to_right = [pair(0, cnt, tgt, 1, 0, right), pair(1, cnt, tgt, 1, 1, right)]
    to_left = [pair(2, cnt, tgt, 2, 0, left), pair(3, cnt, tgt, 2, 1, left)]
    on_right = pair(4, cg.at[1], tg.at[1], 3, 0, right)
    on_left = pair(5, cg.at[2], tg.at[2], 3, 1, left)
    across = {
        (slot, part): pair(6 + 2 * (slot - 1) + part, cg.at[slot], tg.at[slot], slot, part, sibling)
        for slot in (1, 2, 3)
        for part in (0, 1)
    }

    def go(copies):
        for copy in copies:
            copy.start()

    def got(copies):
        for copy in copies:
            copy.wait_recv()

    go(to_right[0])
    go(to_left[1])
    quarter = pl.ds(pl.multiple_of(BLOCK * x, BLOCK), BLOCK)
    mine = pl.ds(pl.multiple_of(BLOCK * j, BLOCK), BLOCK)
    spread = []
    for i, (dz, core) in enumerate([(1, 0), (1, 1), (-1, 0), (-1, 1), (far, 0), (far, 1)]):
        spread.append(remote(frq.at[quarter], fr.at[mine], fsend.at[i], frecv.at[2 * (i // 2) + c], along_z(dz, core)))
    spread.append(remote(frq.at[quarter], fr.at[mine], fsend.at[6], frecv.at[6], sibling))
    go(spread)
    go(to_right[1])
    go(to_left[0])
    local = [
        pltpu.make_async_copy(cnt, cg.at[0], lsem.at[0]),
        pltpu.make_async_copy(tgt, tg.at[0], lsem.at[1]),
        pltpu.make_async_copy(frq.at[quarter], fr.at[mine], lsem.at[2]),
    ]
    go(local)
    got(to_right[0])
    go(on_right)
    go(across[1, 0])
    got(to_left[1])
    go(on_left)
    go(across[2, 1])
    got(to_right[1])
    go(across[1, 1])
    got(to_left[0])
    go(across[2, 0])
    got(on_right)
    go(across[3, 0])
    got(on_left)
    go(across[3, 1])
    for (slot, part), copies in across.items():
        got(twin(6 + 2 * (slot - 1) + part, slot, part))
    for i, (dz, core) in enumerate([(-1, 0), (-1, 1), (1, 0), (1, 1), (-2, 0), (2, 1)]):
        source = along_z(dz, core)
        rows = pl.ds(pl.multiple_of(BLOCK * source[1], BLOCK), BLOCK)
        remote(frq.at[quarter], fr.at[rows], fsend.at[i], frecv.at[2 * (i // 2) + core], source).wait_recv()
    rows = pl.ds(pl.multiple_of(BLOCK * sibling[1], BLOCK), BLOCK)
    remote(frq.at[quarter], fr.at[rows], fsend.at[6], frecv.at[6], sibling).wait_recv()
    for copy in local:
        copy.wait()
    sent = to_right[0] + to_right[1] + to_left[0] + to_left[1] + on_right + on_left + spread
    for copies in across.values():
        sent = sent + copies
    for copy in sent:
        copy.wait_send()


def gather(counters, targets, frequencies):
    bf16 = jnp.bfloat16
    hbm = pl.BlockSpec(memory_space=pl.ANY)
    return pl.pallas_call(
        gather_kernel,
        out_shape=(
            jax.ShapeDtypeStruct((4, ROWS, DEPTH), bf16),
            jax.ShapeDtypeStruct((4, TARGETS, ROWS), bf16),
            jax.ShapeDtypeStruct((8 * BLOCK, DEPTH + 128), bf16),
        ),
        in_specs=[hbm] * 3,
        out_specs=(hbm,) * 3,
        scratch_shapes=[
            pltpu.SemaphoreType.DMA((24,)),
            pltpu.SemaphoreType.DMA((24,)),
            pltpu.SemaphoreType.DMA((7,)),
            pltpu.SemaphoreType.DMA((7,)),
            pltpu.SemaphoreType.DMA((3,)),
        ],
        compiler_params=pltpu.CompilerParams(collective_id=0, has_side_effects=True, vmem_limit_bytes=4 << 20),
        name="gather",
    )(counters, targets, frequencies)


def build_kernel(cnt, tgt, frow, fcol, phase, part, rhs, zrow, gram, right):
    step = pl.program_id(0)
    j = lax.axis_index("feat")

    @pl.when(step == 0)
    def _():
        gram[...] = jnp.zeros_like(gram)
        right[...] = jnp.zeros_like(right)

    nt = (((1,), (1,)), ((), ()))
    rows = cnt[...]
    zcol = cosine(jnp.dot(rows, fcol[...], preferred_element_type=F32) + phase[...].astype(F32))
    mixed = lax.dot_general(frow[:, :DEPTH], rows, nt, preferred_element_type=F32)
    zrow[...] = cosine(mixed + frow[:, DEPTH : DEPTH + 1].astype(F32))
    gram[...] += jnp.dot(zrow[...], zcol, preferred_element_type=F32)
    own = zrow[pl.ds(pl.multiple_of(BLOCK * j, BLOCK), BLOCK), :]
    right[...] += lax.dot_general(tgt[0], own, nt, preferred_element_type=F32)

    @pl.when(step == pl.num_programs(0) - 1)
    def _():
        for block in range(8):
            part[block % 4, block // 4] = gram[block * BLOCK : (block + 1) * BLOCK, :]
        rhs[...] = right[...]


def build(counters, targets, frow, fcol, phases):
    steps = 4 * ROWS // STEP
    per = ROWS // STEP
    whole = lambda shape: pl.BlockSpec(shape, lambda i: (0,) * len(shape))
    return pl.pallas_call(
        build_kernel,
        out_shape=(
            jax.ShapeDtypeStruct((4, 2, BLOCK, WIDTH), F32),
            jax.ShapeDtypeStruct((TARGETS, BLOCK), F32),
        ),
        grid=(steps,),
        in_specs=[
            pl.BlockSpec((STEP, DEPTH), lambda i: (i, 0)),
            pl.BlockSpec((1, TARGETS, STEP), lambda i: (i // per, 0, i % per)),
            whole((8 * BLOCK, DEPTH + 128)),
            whole((DEPTH, WIDTH)),
            whole((1, WIDTH)),
        ],
        out_specs=(whole((4, 2, BLOCK, WIDTH)), whole((TARGETS, BLOCK))),
        scratch_shapes=[
            pltpu.VMEM((8 * BLOCK, STEP), jnp.bfloat16),
            pltpu.VMEM((8 * BLOCK, WIDTH), F32),
            pltpu.VMEM((TARGETS, BLOCK), F32),
        ],
        compiler_params=pltpu.CompilerParams(vmem_limit_bytes=40 << 20),
        name="build",
    )(counters.reshape(4 * ROWS, DEPTH), targets, frow, fcol, phases)


def solve_kernel(
    part, rhs, sol, res, gram,
    ybuf, zsend, zrecv, gother, rh, rj, vj, first, fb, xb, db, w1buf, fin,
    ssem, hsem, rsem, osem, psem, ysem, zsem, gsem, fsem, tsem, xsem, dsem, esem,
):
    s, j = lax.axis_index("samp"), lax.axis_index("feat")
    x, b = lax.rem(s, 4), lax.div(s, 4)
    y, zh = lax.rem(b, 4), lax.div(b, 4)
    c, zl = lax.rem(j, 2), lax.div(j, 2)
    diag = b == j
    sibling = (s, j + 1 - 2 * c)
    xothers = [lax.rem(x + d, 4) for d in (1, 2, 3)]
    xmates = [(b * 4 + o, j) for o in xothers]
    bothers = [lax.rem(b + e, 8) for e in range(1, 8)]
    bmates = [(o * 4 + x, j) for o in bothers]
    fothers = [lax.rem(j + e, 8) for e in range(1, 8)]
    fmates = [(s, o) for o in fothers]
    zothers = [lax.rem(zl + d, 4) for d in (1, 2, 3)]
    zmates = [(s, o * 2 + c) for o in zothers]
    spread_to = [((h * 4 + zl) * 4 + o, lax.div(b, 2) * 2 + c) for h in (0, 1) for o in range(4)]
    spread_from = [((zl * 2 + h) * 4 + o, y * 2 + c) for h in (0, 1) for o in range(4)]
    loop = jnp.logical_and(lax.div(b, 2) == zl, y == zl)

    barrier = pltpu.get_barrier_semaphore()
    for peer in xmates + bmates + fmates:
        pl.semaphore_signal(barrier, inc=1, device_id=peer, device_id_type=MESH)
    for peer in spread_from:

        @pl.when(peer[0] * 8 + peer[1] != s * 8 + j)
        def _(peer=peer):
            pl.semaphore_signal(barrier, inc=1, device_id=peer, device_id_type=MESH)

    pl.semaphore_wait(barrier, jnp.where(loop, 24, 25))

    count = [0]
    sent = []

    def copy(src, dst, recv_sem, device, when=None):
        made = remote(src, dst, ssem.at[count[0]], recv_sem, device)
        count[0] += 1
        sent.append((made, when))
        if when is None:
            made.start()
        else:
            pl.when(when)(made.start)

    def wait(ref, sem):
        remote(ref, ref, ssem.at[0], sem, sibling).wait_recv()

    def lanes(block, size=BLOCK):
        return pl.ds(pl.multiple_of(block * size, size), size)

    half, other_half = pl.ds(32 * c, 32), pl.ds(32 * (1 - c), 32)

    rh[b] = rhs[...]
    for o, peer in zip(bothers, bmates):
        copy(rh.at[b], rh.at[b], hsem.at[b], peer)
    for d in (1, 2, 3):
        to = lax.rem(y + d, 4)
        copy(part.at[to, 1 - zh], ybuf.at[d - 1, 0], ysem.at[d - 1], ((zh * 4 + to) * 4 + x, j))
    for d in (1, 2, 3):
        to = lax.rem(y + d, 4)
        copy(part.at[to, zh], ybuf.at[d - 1, 1], ysem.at[d + 2], ((zh * 4 + to) * 4 + x, j))

    for o in bothers:
        wait(rh.at[o], hsem.at[o])
    total = rh[0]
    for o in range(1, 8):
        total = total + rh[o]
    total = total * (1.0 / math.sqrt(TOTAL))
    rj[:, lanes(x)] = total
    for peer in xmates:
        copy(rj.at[:, lanes(x)], rj.at[:, lanes(x)], rsem.at[x], peer)
    for core in (0, 1):

        @pl.when(jnp.logical_and(diag, c == core))
        def _(core=core):
            first[...] = total[32 * core : 32 * core + 32]

    for o, peer in zip(fothers, fmates):
        copy(rj.at[pl.ds(32 * lax.rem(o, 2), 32), lanes(x)], first, psem, peer, diag)
    for o in xothers:
        wait(rj.at[:, lanes(o)], rsem.at[o])
    for core in (0, 1):

        @pl.when(c == core)
        def _(core=core):
            vj[0, :, core * WIDTH : (core + 1) * WIDTH] = rj[32 * core : 32 * core + 32, :]

    copy(rj.at[other_half, :], vj.at[0, :, lanes(c, WIDTH)], osem, sibling)

    def over_y(which, slot):
        total = part[y, which]
        for d in range(3):
            wait(ybuf.at[d, slot], ysem.at[3 * slot + d])
            total = total + ybuf[d, slot]
        return total

    zsend[...] = over_y(1 - zh, 0)
    copy(zsend, zrecv, zsem, (((1 - zh) * 4 + y) * 4 + x, j))
    gram[...] = over_y(zh, 1)
    wait(vj.at[0, :, lanes(1 - c, WIDTH)], osem)

    @pl.when(jnp.logical_not(diag))
    def _():
        wait(first, psem)

    wait(zrecv, zsem)
    gram[...] = (gram[...] + zrecv[...]) * (1.0 / TOTAL)
    copy(gram, gother, gsem, sibling)

    def multiply(it, wait_gram):
        nt = (((1,), (1,)), ((), ()))
        own = lax.dot_general(vj[it, :, lanes(c, WIDTH)], gram[...], nt, precision=HIGHEST, preferred_element_type=F32)
        if wait_gram:
            wait(gother, gsem)
        fb[it, zl] = own + lax.dot_general(
            vj[it, :, lanes(1 - c, WIDTH)], gother[...], nt, precision=HIGHEST, preferred_element_type=F32
        )
        for peer in zmates:
            copy(fb.at[it, zl], fb.at[it, zl], fsem.at[4 * it + zl], peer)

    def image(it, vector):
        for o in zothers:
            wait(fb.at[it, o], fsem.at[4 * it + o])
        return ((fb[it, 0] + fb[it, 1]) + (fb[it, 2] + fb[it, 3])) + RIDGE * vector

    planes = [(0, 2), (2, 1), (3, 1)]

    def sum_start(k, values):
        p, n = planes[k]
        for i, value in enumerate(values):
            xb[x, p + i] = value
        for peer in xmates:
            copy(xb.at[x, pl.ds(p, n)], xb.at[x, pl.ds(p, n)], xsem.at[4 * k + x], peer)

    def sum_finish(k):
        p, n = planes[k]
        for o in xothers:
            wait(xb.at[o, pl.ds(p, n)], xsem.at[4 * k + o])
        for i in range(p, p + n):
            db[b, i] = (xb[0, i] + xb[1, i]) + (xb[2, i] + xb[3, i])
        for peer in bmates:
            copy(db.at[b, pl.ds(p, n)], db.at[b, pl.ds(p, n)], dsem.at[8 * k + b], peer)
        for o in bothers:
            wait(db.at[o, pl.ds(p, n)], dsem.at[8 * k + o])
        out = []
        for i in range(p, p + n):
            total = db[0, i]
            for o in range(1, 8):
                total = total + db[o, i]
            out.append(jnp.sum(total, axis=1, keepdims=True))
        return out

    multiply(0, True)
    r0 = first[...]
    w1 = image(0, r0)
    w1buf[...] = w1
    place = lax.rem(b, 2) * 4 + x
    for peer in spread_to:
        copy(w1buf, vj.at[1, :, lanes(place)], tsem.at[place], peer, peer[0] * 8 + peer[1] != s * 8 + j)

    @pl.when(loop)
    def _():
        vj[1, :, lanes(place)] = w1

    sum_start(0, [r0 * r0, r0 * w1])
    for i, peer in enumerate(spread_from):

        @pl.when(peer[0] * 8 + peer[1] != s * 8 + j)
        def _(i=i):
            wait(vj.at[1, :, BLOCK * i : BLOCK * (i + 1)], tsem.at[i])

    multiply(1, False)
    rr0, curve0 = sum_finish(0)
    a0 = rr0 / curve0
    r1 = r0 - a0 * w1
    sum_start(1, [r1 * r1])
    (rr1,) = sum_finish(1)
    b0 = rr1 / rr0
    d1 = r1 + b0 * r0
    w2 = image(1, w1)
    image1 = (w1 - a0 * w2) + b0 * w1
    sum_start(2, [d1 * image1])
    (curve1,) = sum_finish(2)
    a1 = rr1 / curve1
    for core in (0, 1):

        @pl.when(c == core)
        def _(core=core):
            fin[0, 32 * core : 32 * core + 32] = a0 * r0 + a1 * d1
            fin[1, 32 * core : 32 * core + 32] = r1 - a1 * image1

    copy(fin.at[:, half], fin.at[:, half], esem, sibling)
    wait(fin.at[:, other_half], esem)
    sol[...] = fin[0]
    res[...] = fin[1]
    for made, when in sent:
        if when is None:
            made.wait_send()
        else:
            pl.when(when)(made.wait_send)


def solve(part, rhs):
    vmem = pl.BlockSpec(memory_space=pltpu.VMEM)
    dma = pltpu.SemaphoreType.DMA
    vector, some = (TARGETS, BLOCK), (TARGETS // 2, BLOCK)
    shapes = [
        (3, 2, BLOCK, WIDTH), (BLOCK, WIDTH), (BLOCK, WIDTH), (BLOCK, WIDTH), (8,) + vector, (TARGETS, WIDTH),
        (2, TARGETS // 2, 2 * WIDTH), some, (2, 4) + some, (4, 4) + some, (8, 4) + some, some, (2,) + vector,
    ]
    return pl.pallas_call(
        solve_kernel,
        out_shape=(
            jax.ShapeDtypeStruct(vector, F32),
            jax.ShapeDtypeStruct(vector, F32),
            jax.ShapeDtypeStruct((BLOCK, WIDTH), F32),
        ),
        in_specs=[vmem] * 2,
        out_specs=(vmem,) * 3,
        scratch_shapes=[pltpu.VMEM(shape, F32) for shape in shapes]
        + [
            dma((80,)), dma((8,)), dma((4,)), dma, dma, dma((6,)), dma, dma, dma((8,)), dma((8,)),
            dma((12,)), dma((24,)), dma,
        ],
        compiler_params=pltpu.CompilerParams(collective_id=1, has_side_effects=True, vmem_limit_bytes=24 << 20),
        name="solve",
    )(part, rhs)


def on_device(counters, frequencies, phases, targets):
    columns = jnp.concatenate([frequencies.T, jnp.broadcast_to(phases.T, (WIDTH, 128))], axis=1)
    all_counters, all_targets, rows = gather(counters, targets.T, columns)
    part, rhs = build(all_counters, all_targets, rows, frequencies, phases)
    solution, residual, gram = solve(part, rhs)
    return solution.T, residual.T, gram


def solution(mesh):
    return jax.shard_map(
        on_device,
        mesh=mesh,
        in_specs=(P("samp", None), P(None, "feat"), P(None, "feat"), P("samp", None)),
        out_specs=(P("samp", None), P("samp", None), P("samp", "feat")),
        check_vma=False,
    )
```

```python
import math

import jax
import jax.numpy as jnp
from jax import lax
from jax.experimental import pallas as pl
from jax.experimental.pallas import tpu as pltpu
from jax.sharding import PartitionSpec as P

RIDGE = 0.05
ROWS, DEPTH, WIDTH, TARGETS, BLOCK = 1024, 512, 512, 64, 128
TOTAL = 32768
STEP = 512
MESH = pl.DeviceIdType.MESH
SINE = (4.442883014678955, -7.308241367340088, 3.6062889099121094, -0.8457635641098022, 0.10920573770999908)
HIGHEST = lax.Precision.HIGHEST
F32 = jnp.float32


def cosine(angle):
    turns = angle * (0.5 / math.pi)
    f = turns - jnp.round(turns)
    square = f * f
    poly = SINE[-1]
    for coefficient in SINE[-2::-1]:
        poly = poly * square + coefficient
    root = poly * f
    return (1.0 - root * root).astype(jnp.bfloat16)


def remote(src, dst, send_sem, recv_sem, device):
    return pltpu.make_async_remote_copy(
        src_ref=src, dst_ref=dst, send_sem=send_sem, recv_sem=recv_sem, device_id=device, device_id_type=MESH
    )


def greet(peers):
    barrier = pltpu.get_barrier_semaphore()
    for peer in peers:
        pl.semaphore_signal(barrier, inc=1, device_id=peer, device_id_type=MESH)
    pl.semaphore_wait(barrier, len(peers))


def gather_kernel(cnt, tgt, frq, cg, tg, fr, ssem, rsem, fsend, frecv, lsem):
    s, j = lax.axis_index("samp"), lax.axis_index("feat")
    x, c, zl, zh = lax.rem(s, 4), lax.rem(j, 2), lax.div(j, 2), lax.div(s, 16)
    z = zh * 4 + zl
    right = (s - x + lax.rem(x + 1, 4), j)
    left = (s - x + lax.rem(x + 3, 4), j)
    sibling = (s, j + 1 - 2 * c)

    def along_z(dz, core):
        other = lax.rem(z + dz + 8, 8)
        return (lax.div(other, 4) * 16 + lax.rem(s, 16), lax.rem(other, 4) * 2 + core)

    far = 2 - 4 * c
    greet(
        [right, left, sibling]
        + [along_z(dz, core) for dz in (1, -1) for core in (0, 1)]
        + [along_z(far, 0), along_z(far, 1), along_z(-far, c)]
    )

    half = STEP * c
    a_rows, b_rows = pl.ds(pl.multiple_of(half, 256), 256), pl.ds(pl.multiple_of(half + 256, 256), 256)
    a_cols = pl.ds(pl.multiple_of(half, 256), 256)
    b_cols = pl.ds(pl.multiple_of(half + 256, 256), 256)

    def pair(i, src_c, src_t, slot, part, device):
        rows, cols = (a_rows, a_cols) if part == 0 else (b_rows, b_cols)
        return [
            remote(src_c.at[rows], cg.at[slot, rows], ssem.at[2 * i], rsem.at[2 * i], device),
            remote(src_t.at[:, cols], tg.at[slot, :, cols], ssem.at[2 * i + 1], rsem.at[2 * i + 1], device),
        ]

    def twin(i, slot, part):
        other = STEP - half
        rows = pl.ds(pl.multiple_of(other + 256 * part, 256), 256)
        cols = pl.ds(pl.multiple_of(other + 256 * part, 256), 256)
        return [
            remote(cg.at[slot, rows], cg.at[slot, rows], ssem.at[2 * i], rsem.at[2 * i], sibling),
            remote(tg.at[slot, :, cols], tg.at[slot, :, cols], ssem.at[2 * i + 1], rsem.at[2 * i + 1], sibling),
        ]

    to_right = [pair(0, cnt, tgt, 1, 0, right), pair(1, cnt, tgt, 1, 1, right)]
    to_left = [pair(2, cnt, tgt, 2, 0, left), pair(3, cnt, tgt, 2, 1, left)]
    on_right = pair(4, cg.at[1], tg.at[1], 3, 0, right)
    on_left = pair(5, cg.at[2], tg.at[2], 3, 1, left)
    across = {
        (slot, part): pair(6 + 2 * (slot - 1) + part, cg.at[slot], tg.at[slot], slot, part, sibling)
        for slot in (1, 2, 3)
        for part in (0, 1)
    }

    def go(copies):
        for copy in copies:
            copy.start()

    def got(copies):
        for copy in copies:
            copy.wait_recv()

    go(to_right[0])
    go(to_left[1])
    quarter = pl.ds(pl.multiple_of(BLOCK * x, BLOCK), BLOCK)
    mine = pl.ds(pl.multiple_of(BLOCK * j, BLOCK), BLOCK)
    spread = []
    for i, (dz, core) in enumerate([(1, 0), (1, 1), (-1, 0), (-1, 1), (far, 0), (far, 1)]):
        spread.append(remote(frq.at[quarter], fr.at[mine], fsend.at[i], frecv.at[2 * (i // 2) + c], along_z(dz, core)))
    spread.append(remote(frq.at[quarter], fr.at[mine], fsend.at[6], frecv.at[6], sibling))
    go(spread)
    go(to_right[1])
    go(to_left[0])
    local = [
        pltpu.make_async_copy(cnt, cg.at[0], lsem.at[0]),
        pltpu.make_async_copy(tgt, tg.at[0], lsem.at[1]),
        pltpu.make_async_copy(frq.at[quarter], fr.at[mine], lsem.at[2]),
    ]
    go(local)
    got(to_right[0])
    go(on_right)
    go(across[1, 0])
    got(to_left[1])
    go(on_left)
    go(across[2, 1])
    got(to_right[1])
    go(across[1, 1])
    got(to_left[0])
    go(across[2, 0])
    got(on_right)
    go(across[3, 0])
    got(on_left)
    go(across[3, 1])
    for (slot, part), copies in across.items():
        got(twin(6 + 2 * (slot - 1) + part, slot, part))
    for i, (dz, core) in enumerate([(-1, 0), (-1, 1), (1, 0), (1, 1), (-2, 0), (2, 1)]):
        source = along_z(dz, core)
        rows = pl.ds(pl.multiple_of(BLOCK * source[1], BLOCK), BLOCK)
        remote(frq.at[quarter], fr.at[rows], fsend.at[i], frecv.at[2 * (i // 2) + core], source).wait_recv()
    rows = pl.ds(pl.multiple_of(BLOCK * sibling[1], BLOCK), BLOCK)
    remote(frq.at[quarter], fr.at[rows], fsend.at[6], frecv.at[6], sibling).wait_recv()
    for copy in local:
        copy.wait()
    sent = to_right[0] + to_right[1] + to_left[0] + to_left[1] + on_right + on_left + spread
    for copies in across.values():
        sent = sent + copies
    for copy in sent:
        copy.wait_send()


def gather(counters, targets, frequencies):
    bf16 = jnp.bfloat16
    hbm = pl.BlockSpec(memory_space=pl.ANY)
    return pl.pallas_call(
        gather_kernel,
        out_shape=(
            jax.ShapeDtypeStruct((4, ROWS, DEPTH), bf16),
            jax.ShapeDtypeStruct((4, TARGETS, ROWS), bf16),
            jax.ShapeDtypeStruct((8 * BLOCK, DEPTH + 128), bf16),
        ),
        in_specs=[hbm] * 3,
        out_specs=(hbm,) * 3,
        scratch_shapes=[
            pltpu.SemaphoreType.DMA((24,)),
            pltpu.SemaphoreType.DMA((24,)),
            pltpu.SemaphoreType.DMA((7,)),
            pltpu.SemaphoreType.DMA((7,)),
            pltpu.SemaphoreType.DMA((3,)),
        ],
        compiler_params=pltpu.CompilerParams(collective_id=0, has_side_effects=True, vmem_limit_bytes=4 << 20),
        name="gather",
    )(counters, targets, frequencies)


def build_kernel(cnt, tgt, frow, fcol, phase, part, rhs, zrow, gram, right):
    step = pl.program_id(0)
    j = lax.axis_index("feat")

    @pl.when(step == 0)
    def _():
        gram[...] = jnp.zeros_like(gram)
        right[...] = jnp.zeros_like(right)

    nt = (((1,), (1,)), ((), ()))
    rows = cnt[...]
    zcol = cosine(jnp.dot(rows, fcol[...], preferred_element_type=F32) + phase[...].astype(F32))
    mixed = lax.dot_general(frow[:, :DEPTH], rows, nt, preferred_element_type=F32)
    zrow[...] = cosine(mixed + frow[:, DEPTH : DEPTH + 1].astype(F32))
    gram[...] += jnp.dot(zrow[...], zcol, preferred_element_type=F32)
    own = zrow[pl.ds(pl.multiple_of(BLOCK * j, BLOCK), BLOCK), :]
    right[...] += lax.dot_general(tgt[0], own, nt, preferred_element_type=F32)

    @pl.when(step == pl.num_programs(0) - 1)
    def _():
        for block in range(8):
            part[block % 4, block // 4] = gram[block * BLOCK : (block + 1) * BLOCK, :]
        rhs[...] = right[...]


def build(counters, targets, frow, fcol, phases):
    steps = 4 * ROWS // STEP
    per = ROWS // STEP
    whole = lambda shape: pl.BlockSpec(shape, lambda i: (0,) * len(shape))
    return pl.pallas_call(
        build_kernel,
        out_shape=(
            jax.ShapeDtypeStruct((4, 2, BLOCK, WIDTH), F32),
            jax.ShapeDtypeStruct((TARGETS, BLOCK), F32),
        ),
        grid=(steps,),
        in_specs=[
            pl.BlockSpec((STEP, DEPTH), lambda i: (i, 0)),
            pl.BlockSpec((1, TARGETS, STEP), lambda i: (i // per, 0, i % per)),
            whole((8 * BLOCK, DEPTH + 128)),
            whole((DEPTH, WIDTH)),
            whole((1, WIDTH)),
        ],
        out_specs=(whole((4, 2, BLOCK, WIDTH)), whole((TARGETS, BLOCK))),
        scratch_shapes=[
            pltpu.VMEM((8 * BLOCK, STEP), jnp.bfloat16),
            pltpu.VMEM((8 * BLOCK, WIDTH), F32),
            pltpu.VMEM((TARGETS, BLOCK), F32),
        ],
        compiler_params=pltpu.CompilerParams(vmem_limit_bytes=40 << 20),
        name="build",
    )(counters.reshape(4 * ROWS, DEPTH), targets, frow, fcol, phases)


def solve_kernel(
    part, rhs, sol, res, gram,
    ybuf, zsend, zrecv, gother, rh, rj, vj, first, fb, sums, w1buf, fin,
    ssem, hsem, rsem, osem, psem, ysem, zsem, gsem, fsem, tsem, xsem, esem,
):
    s, j = lax.axis_index("samp"), lax.axis_index("feat")
    x, b = lax.rem(s, 4), lax.div(s, 4)
    y, zh = lax.rem(b, 4), lax.div(b, 4)
    c, zl = lax.rem(j, 2), lax.div(j, 2)
    diag = b == j
    sibling = (s, j + 1 - 2 * c)
    xothers = [lax.rem(x + d, 4) for d in (1, 2, 3)]
    xmates = [(b * 4 + o, j) for o in xothers]
    bothers = [lax.rem(b + e, 8) for e in range(1, 8)]
    bmates = [(o * 4 + x, j) for o in bothers]
    fothers = [lax.rem(j + e, 8) for e in range(1, 8)]
    fmates = [(s, o) for o in fothers]
    zothers = [lax.rem(zl + d, 4) for d in (1, 2, 3)]
    zmates = [(s, o * 2 + c) for o in zothers]
    yothers = [lax.rem(y + d, 4) for d in (1, 2, 3)]
    ymates = [((zh * 4 + o) * 4 + x, j) for o in yothers]
    z = zh * 4 + zl
    rothers = [lax.rem(z + e, 8) for e in range(1, 8)]
    rmates = [((lax.div(o, 4) * 4 + y) * 4 + x, lax.rem(o, 4) * 2 + c) for o in rothers]
    across = [((1 - zh) * 16 + y * 4 + x, o * 2 + c) for o in zothers]
    down = lax.div(b, 2)
    same = lax.div(zl, 2) == zh
    near = jnp.where(same, zl == down, zl == 3 * (1 - zh))
    to_zh = jnp.where(same, zh, 1 - zh)
    skip = jnp.where(near, 2, 0)
    spread_to = [((to_zh * 4 + lax.rem(y + skip + d, 4)) * 4 + o, down * 2 + c) for d in (0, 1) for o in range(4)]
    spread_from = []
    for h in (0, 1):
        source_y, source_zh = lax.rem(zl, 2) * 2 + h, lax.div(zl, 2)
        far = jnp.where(lax.rem(y + 4 - source_y, 4) < 2, 1, 0)
        inside = zl + far * (1 - 2 * lax.rem(zl, 2))
        outside = jnp.where(source_zh == 0, 3 - far, far)
        source_zl = jnp.where(zh == source_zh, inside, outside)
        spread_from += [((zl * 2 + h) * 4 + o, source_zl * 2 + c) for o in range(4)]

    barrier = pltpu.get_barrier_semaphore()
    peers = xmates + bmates + fmates + across + spread_from
    for peer in peers:
        pl.semaphore_signal(barrier, inc=1, device_id=peer, device_id_type=MESH)
    pl.semaphore_wait(barrier, len(peers))

    count = [0]
    sent = []

    def copy(src, dst, recv_sem, device, when=None):
        made = remote(src, dst, ssem.at[count[0]], recv_sem, device)
        count[0] += 1
        sent.append((made, when))
        if when is None:
            made.start()
        else:
            pl.when(when)(made.start)

    def wait(ref, sem):
        remote(ref, ref, ssem.at[0], sem, sibling).wait_recv()

    def lanes(block, size=BLOCK):
        return pl.ds(pl.multiple_of(block * size, size), size)

    half, other_half = pl.ds(32 * c, 32), pl.ds(32 * (1 - c), 32)

    rh[b] = rhs[...]
    for o, peer in zip(bothers, bmates):
        copy(rh.at[b], rh.at[b], hsem.at[b], peer)
    for d in (1, 2, 3):
        to = lax.rem(y + d, 4)
        copy(part.at[to, 1 - zh], ybuf.at[d - 1, 0], ysem.at[d - 1], ((zh * 4 + to) * 4 + x, j))
    for d in (1, 2, 3):
        to = lax.rem(y + d, 4)
        copy(part.at[to, zh], ybuf.at[d - 1, 1], ysem.at[d + 2], ((zh * 4 + to) * 4 + x, j))

    for o in bothers:
        wait(rh.at[o], hsem.at[o])
    total = rh[0]
    for o in range(1, 8):
        total = total + rh[o]
    total = total * (1.0 / math.sqrt(TOTAL))
    rj[:, lanes(x)] = total
    for peer in xmates:
        copy(rj.at[:, lanes(x)], rj.at[:, lanes(x)], rsem.at[x], peer)
    for core in (0, 1):

        @pl.when(jnp.logical_and(diag, c == core))
        def _(core=core):
            first[...] = total[32 * core : 32 * core + 32]

    for o, peer in zip(fothers, fmates):
        copy(rj.at[pl.ds(32 * lax.rem(o, 2), 32), lanes(x)], first, psem, peer, diag)
    for o in xothers:
        wait(rj.at[:, lanes(o)], rsem.at[o])
    for core in (0, 1):

        @pl.when(c == core)
        def _(core=core):
            vj[0, :, core * WIDTH : (core + 1) * WIDTH] = rj[32 * core : 32 * core + 32, :]

    copy(rj.at[other_half, :], vj.at[0, :, lanes(c, WIDTH)], osem, sibling)

    def over_y(which, slot):
        total = part[y, which]
        for d in range(3):
            wait(ybuf.at[d, slot], ysem.at[3 * slot + d])
            total = total + ybuf[d, slot]
        return total

    zsend[...] = over_y(1 - zh, 0)
    copy(zsend, zrecv, zsem, (((1 - zh) * 4 + y) * 4 + x, j))
    gram[...] = over_y(zh, 1)
    wait(vj.at[0, :, lanes(1 - c, WIDTH)], osem)

    @pl.when(jnp.logical_not(diag))
    def _():
        wait(first, psem)

    wait(zrecv, zsem)
    gram[...] = (gram[...] + zrecv[...]) * (1.0 / TOTAL)
    copy(gram, gother, gsem, sibling)

    def multiply(it, wait_gram):
        nt = (((1,), (1,)), ((), ()))
        own = lax.dot_general(vj[it, :, lanes(c, WIDTH)], gram[...], nt, precision=HIGHEST, preferred_element_type=F32)
        if wait_gram:
            wait(gother, gsem)
        fb[it, zl] = own + lax.dot_general(
            vj[it, :, lanes(1 - c, WIDTH)], gother[...], nt, precision=HIGHEST, preferred_element_type=F32
        )
        for peer in zmates:
            copy(fb.at[it, zl], fb.at[it, zl], fsem.at[4 * it + zl], peer)

    def image(it, vector):
        for o in zothers:
            wait(fb.at[it, o], fsem.at[4 * it + o])
        return ((fb[it, 0] + fb[it, 1]) + (fb[it, 2] + fb[it, 3])) + RIDGE * vector

    some = (TARGETS // 2, BLOCK)
    match = lax.broadcasted_iota(jnp.int32, some, 0) == lax.broadcasted_iota(jnp.int32, some, 1)
    sublane = lax.broadcasted_iota(jnp.int32, (8, BLOCK), 0)

    def pack(values):
        tile = jnp.zeros((8, BLOCK), F32)
        for i, value in enumerate(values):
            sums = jnp.where(match, jnp.sum(value, axis=1, keepdims=True), 0.0)
            tile = jnp.where(sublane == i, jnp.sum(sums, axis=0, keepdims=True), tile)
        return tile

    def unpack(tile, i):
        return jnp.sum(jnp.where(match, tile[i : i + 1], 0.0), axis=1, keepdims=True)

    def share(base, mine, mates, tile):
        sums[base + mine] = tile
        for peer in mates:
            copy(sums.at[base + mine], sums.at[base + mine], xsem.at[base + mine], peer)

    def shared(base, others):
        for o in others:
            wait(sums.at[base + o], xsem.at[base + o])
        total = sums[base]
        for i in range(1, len(others) + 1):
            total = total + sums[base + i]
        return total

    multiply(0, True)
    r0 = first[...]
    w1 = image(0, r0)
    w1buf[...] = w1
    place = lax.rem(b, 2) * 4 + x
    for peer in spread_to:
        copy(w1buf, vj.at[1, :, lanes(place)], tsem.at[place], peer)
    share(0, x, xmates, pack([r0 * r0, r0 * w1, w1 * w1]))
    share(4, b, bmates, shared(0, xothers))
    for i in range(8):
        wait(vj.at[1, :, BLOCK * i : BLOCK * (i + 1)], tsem.at[i])
    multiply(1, False)
    tile = shared(4, bothers)
    rr0, curve0, square = (unpack(tile, i) for i in range(3))
    a0 = rr0 / curve0
    mu = square / curve0
    r1 = r0 - a0 * w1
    u = w1 - mu * r0
    piece = fb[1, zl] - (0.25 * (mu - RIDGE)) * w1
    share(12, x, xmates, pack([u * piece, 0.25 * (r1 * u)]))
    share(16, y, ymates, shared(12, xothers))
    share(20, z, rmates, shared(16, yothers))
    image1 = image(1, w1) - mu * w1
    tile = shared(20, rothers)
    tau = unpack(tile, 1) / unpack(tile, 0)
    for core in (0, 1):

        @pl.when(c == core)
        def _(core=core):
            fin[0, 32 * core : 32 * core + 32] = a0 * r0 + tau * u
            fin[1, 32 * core : 32 * core + 32] = r1 - tau * image1

    copy(fin.at[:, half], fin.at[:, half], esem, sibling)
    wait(fin.at[:, other_half], esem)
    sol[...] = fin[0]
    res[...] = fin[1]
    for made, when in sent:
        if when is None:
            made.wait_send()
        else:
            pl.when(when)(made.wait_send)


def solve(part, rhs):
    vmem = pl.BlockSpec(memory_space=pltpu.VMEM)
    dma = pltpu.SemaphoreType.DMA
    vector, some = (TARGETS, BLOCK), (TARGETS // 2, BLOCK)
    shapes = [
        (3, 2, BLOCK, WIDTH), (BLOCK, WIDTH), (BLOCK, WIDTH), (BLOCK, WIDTH), (8,) + vector, (TARGETS, WIDTH),
        (2, TARGETS // 2, 2 * WIDTH), some, (2, 4) + some, (28, 8, BLOCK), some, (2,) + vector,
    ]
    return pl.pallas_call(
        solve_kernel,
        out_shape=(
            jax.ShapeDtypeStruct(vector, F32),
            jax.ShapeDtypeStruct(vector, F32),
            jax.ShapeDtypeStruct((BLOCK, WIDTH), F32),
        ),
        in_specs=[vmem] * 2,
        out_specs=(vmem,) * 3,
        scratch_shapes=[pltpu.VMEM(shape, F32) for shape in shapes]
        + [
            dma((96,)), dma((8,)), dma((4,)), dma, dma, dma((6,)), dma, dma, dma((8,)), dma((8,)),
            dma((28,)), dma,
        ],
        compiler_params=pltpu.CompilerParams(collective_id=1, has_side_effects=True, vmem_limit_bytes=24 << 20),
        name="solve",
    )(part, rhs)


def on_device(counters, frequencies, phases, targets):
    columns = jnp.concatenate([frequencies.T, jnp.broadcast_to(phases.T, (WIDTH, 128))], axis=1)
    all_counters, all_targets, rows = gather(counters, targets.T, columns)
    part, rhs = build(all_counters, all_targets, rows, frequencies, phases)
    solution, residual, gram = solve(part, rhs)
    return solution.T, residual.T, gram


def solution(mesh):
    return jax.shard_map(
        on_device,
        mesh=mesh,
        in_specs=(P("samp", None), P(None, "feat"), P(None, "feat"), P("samp", None)),
        out_specs=(P("samp", None), P("samp", None), P("samp", "feat")),
        check_vma=False,
    )
```

```python
import math

import jax
import jax.numpy as jnp
from jax import lax
from jax.experimental import pallas as pl
from jax.experimental.pallas import tpu as pltpu
from jax.sharding import PartitionSpec as P

RIDGE = 0.05
ROWS, DEPTH, WIDTH, TARGETS, BLOCK = 1024, 512, 512, 64, 128
TOTAL = 32768
STEP = 512
MESH = pl.DeviceIdType.MESH
SINE = (4.442883014678955, -7.308241367340088, 3.6062889099121094, -0.8457635641098022, 0.10920573770999908)
HIGHEST = lax.Precision.HIGHEST
F32 = jnp.float32


def cosine(angle):
    turns = angle * (0.5 / math.pi)
    f = turns - jnp.round(turns)
    square = f * f
    poly = SINE[-1]
    for coefficient in SINE[-2::-1]:
        poly = poly * square + coefficient
    root = poly * f
    return (1.0 - root * root).astype(jnp.bfloat16)


def remote(src, dst, send_sem, recv_sem, device):
    return pltpu.make_async_remote_copy(
        src_ref=src, dst_ref=dst, send_sem=send_sem, recv_sem=recv_sem, device_id=device, device_id_type=MESH
    )


def greet(peers):
    barrier = pltpu.get_barrier_semaphore()
    for peer in peers:
        pl.semaphore_signal(barrier, inc=1, device_id=peer, device_id_type=MESH)
    pl.semaphore_wait(barrier, len(peers))


def gather_kernel(cnt, tgt, frq, cg, tg, fr, ssem, rsem, fsend, frecv, lsem):
    s, j = lax.axis_index("samp"), lax.axis_index("feat")
    x, c, zl, zh = lax.rem(s, 4), lax.rem(j, 2), lax.div(j, 2), lax.div(s, 16)
    z = zh * 4 + zl
    right = (s - x + lax.rem(x + 1, 4), j)
    left = (s - x + lax.rem(x + 3, 4), j)
    sibling = (s, j + 1 - 2 * c)

    def along_z(dz, core):
        other = lax.rem(z + dz + 8, 8)
        return (lax.div(other, 4) * 16 + lax.rem(s, 16), lax.rem(other, 4) * 2 + core)

    far = 2 - 4 * c
    greet(
        [right, left, sibling]
        + [along_z(dz, core) for dz in (1, -1) for core in (0, 1)]
        + [along_z(far, 0), along_z(far, 1), along_z(-far, c)]
    )

    half = STEP * c
    a_rows, b_rows = pl.ds(pl.multiple_of(half, 256), 256), pl.ds(pl.multiple_of(half + 256, 256), 256)
    a_cols = pl.ds(pl.multiple_of(half, 256), 256)
    b_cols = pl.ds(pl.multiple_of(half + 256, 256), 256)

    def pair(i, src_c, src_t, slot, part, device):
        rows, cols = (a_rows, a_cols) if part == 0 else (b_rows, b_cols)
        return [
            remote(src_c.at[rows], cg.at[slot, rows], ssem.at[2 * i], rsem.at[2 * i], device),
            remote(src_t.at[:, cols], tg.at[slot, :, cols], ssem.at[2 * i + 1], rsem.at[2 * i + 1], device),
        ]

    def twin(i, slot, part):
        other = STEP - half
        rows = pl.ds(pl.multiple_of(other + 256 * part, 256), 256)
        cols = pl.ds(pl.multiple_of(other + 256 * part, 256), 256)
        return [
            remote(cg.at[slot, rows], cg.at[slot, rows], ssem.at[2 * i], rsem.at[2 * i], sibling),
            remote(tg.at[slot, :, cols], tg.at[slot, :, cols], ssem.at[2 * i + 1], rsem.at[2 * i + 1], sibling),
        ]

    to_right = [pair(0, cnt, tgt, 1, 0, right), pair(1, cnt, tgt, 1, 1, right)]
    to_left = [pair(2, cnt, tgt, 2, 0, left), pair(3, cnt, tgt, 2, 1, left)]
    on_right = pair(4, cg.at[1], tg.at[1], 3, 0, right)
    on_left = pair(5, cg.at[2], tg.at[2], 3, 1, left)
    across = {
        (slot, part): pair(6 + 2 * (slot - 1) + part, cg.at[slot], tg.at[slot], slot, part, sibling)
        for slot in (1, 2, 3)
        for part in (0, 1)
    }

    def go(copies):
        for copy in copies:
            copy.start()

    def got(copies):
        for copy in copies:
            copy.wait_recv()

    go(to_right[0])
    go(to_left[1])
    quarter = pl.ds(pl.multiple_of(BLOCK * x, BLOCK), BLOCK)
    mine = pl.ds(pl.multiple_of(BLOCK * j, BLOCK), BLOCK)
    spread = []
    for i, (dz, core) in enumerate([(1, 0), (1, 1), (-1, 0), (-1, 1), (far, 0), (far, 1)]):
        spread.append(remote(frq.at[quarter], fr.at[mine], fsend.at[i], frecv.at[2 * (i // 2) + c], along_z(dz, core)))
    spread.append(remote(frq.at[quarter], fr.at[mine], fsend.at[6], frecv.at[6], sibling))
    go(spread)
    go(to_right[1])
    go(to_left[0])
    local = [
        pltpu.make_async_copy(cnt, cg.at[0], lsem.at[0]),
        pltpu.make_async_copy(tgt, tg.at[0], lsem.at[1]),
        pltpu.make_async_copy(frq.at[quarter], fr.at[mine], lsem.at[2]),
    ]
    go(local)
    got(to_right[0])
    go(on_right)
    go(across[1, 0])
    got(to_left[1])
    go(on_left)
    go(across[2, 1])
    got(to_right[1])
    go(across[1, 1])
    got(to_left[0])
    go(across[2, 0])
    got(on_right)
    go(across[3, 0])
    got(on_left)
    go(across[3, 1])
    for (slot, part), copies in across.items():
        got(twin(6 + 2 * (slot - 1) + part, slot, part))
    for i, (dz, core) in enumerate([(-1, 0), (-1, 1), (1, 0), (1, 1), (-2, 0), (2, 1)]):
        source = along_z(dz, core)
        rows = pl.ds(pl.multiple_of(BLOCK * source[1], BLOCK), BLOCK)
        remote(frq.at[quarter], fr.at[rows], fsend.at[i], frecv.at[2 * (i // 2) + core], source).wait_recv()
    rows = pl.ds(pl.multiple_of(BLOCK * sibling[1], BLOCK), BLOCK)
    remote(frq.at[quarter], fr.at[rows], fsend.at[6], frecv.at[6], sibling).wait_recv()
    for copy in local:
        copy.wait()
    sent = to_right[0] + to_right[1] + to_left[0] + to_left[1] + on_right + on_left + spread
    for copies in across.values():
        sent = sent + copies
    for copy in sent:
        copy.wait_send()


def gather(counters, targets, frequencies):
    bf16 = jnp.bfloat16
    hbm = pl.BlockSpec(memory_space=pl.ANY)
    return pl.pallas_call(
        gather_kernel,
        out_shape=(
            jax.ShapeDtypeStruct((4, ROWS, DEPTH), bf16),
            jax.ShapeDtypeStruct((4, TARGETS, ROWS), bf16),
            jax.ShapeDtypeStruct((8 * BLOCK, DEPTH + 128), bf16),
        ),
        in_specs=[hbm] * 3,
        out_specs=(hbm,) * 3,
        scratch_shapes=[
            pltpu.SemaphoreType.DMA((24,)),
            pltpu.SemaphoreType.DMA((24,)),
            pltpu.SemaphoreType.DMA((7,)),
            pltpu.SemaphoreType.DMA((7,)),
            pltpu.SemaphoreType.DMA((3,)),
        ],
        compiler_params=pltpu.CompilerParams(collective_id=0, has_side_effects=True, vmem_limit_bytes=4 << 20),
        name="gather",
    )(counters, targets, frequencies)


def solve_kernel(
    cnt, tgt, frow, fcol, phase, sol, res, gram,
    zcol, right, pair, acc, part, ybuf, zsend, zrecv, gother, rh, rj, vj, first, fb, sums, w1buf, fin,
    ssem, hsem, rsem, osem, psem, ysem, zsem, gsem, fsem, tsem, xsem, esem,
):
    s, j = lax.axis_index("samp"), lax.axis_index("feat")
    x, b = lax.rem(s, 4), lax.div(s, 4)
    y, zh = lax.rem(b, 4), lax.div(b, 4)
    c, zl = lax.rem(j, 2), lax.div(j, 2)
    diag = b == j
    sibling = (s, j + 1 - 2 * c)
    xothers = [lax.rem(x + d, 4) for d in (1, 2, 3)]
    xmates = [(b * 4 + o, j) for o in xothers]
    bothers = [lax.rem(b + e, 8) for e in range(1, 8)]
    bmates = [(o * 4 + x, j) for o in bothers]
    fothers = [lax.rem(j + e, 8) for e in range(1, 8)]
    fmates = [(s, o) for o in fothers]
    zothers = [lax.rem(zl + d, 4) for d in (1, 2, 3)]
    zmates = [(s, o * 2 + c) for o in zothers]
    yothers = [lax.rem(y + d, 4) for d in (1, 2, 3)]
    ymates = [((zh * 4 + o) * 4 + x, j) for o in yothers]
    z = zh * 4 + zl
    rothers = [lax.rem(z + e, 8) for e in range(1, 8)]
    rmates = [((lax.div(o, 4) * 4 + y) * 4 + x, lax.rem(o, 4) * 2 + c) for o in rothers]
    across = [((1 - zh) * 16 + y * 4 + x, o * 2 + c) for o in zothers]
    down = lax.div(b, 2)
    same = lax.div(zl, 2) == zh
    near = jnp.where(same, zl == down, zl == 3 * (1 - zh))
    to_zh = jnp.where(same, zh, 1 - zh)
    skip = jnp.where(near, 2, 0)
    spread_to = [((to_zh * 4 + lax.rem(y + skip + d, 4)) * 4 + o, down * 2 + c) for d in (0, 1) for o in range(4)]
    spread_from = []
    for h in (0, 1):
        source_y, source_zh = lax.rem(zl, 2) * 2 + h, lax.div(zl, 2)
        far = jnp.where(lax.rem(y + 4 - source_y, 4) < 2, 1, 0)
        inside = zl + far * (1 - 2 * lax.rem(zl, 2))
        outside = jnp.where(source_zh == 0, 3 - far, far)
        source_zl = jnp.where(zh == source_zh, inside, outside)
        spread_from += [((zl * 2 + h) * 4 + o, source_zl * 2 + c) for o in range(4)]

    barrier = pltpu.get_barrier_semaphore()
    peers = xmates + bmates + fmates + across + spread_from
    for peer in peers:
        pl.semaphore_signal(barrier, inc=1, device_id=peer, device_id_type=MESH)

    nt = (((1,), (1,)), ((), ()))
    right[...] = jnp.zeros_like(right)

    def features(block, rows):
        mixed = lax.dot_general(block[:, :DEPTH], rows, nt, preferred_element_type=F32)
        return cosine(mixed + block[:, DEPTH : DEPTH + 1].astype(F32))

    @pl.loop(0, 4 * ROWS // STEP)
    def _(i):
        chunk = pl.ds(pl.multiple_of(i * STEP, STEP), STEP)
        rows = cnt[chunk, :]
        zcol[chunk, :] = cosine(jnp.dot(rows, fcol[...], preferred_element_type=F32) + phase[...].astype(F32))
        own = features(frow[pl.ds(pl.multiple_of(BLOCK * j, BLOCK), BLOCK), :], rows)
        columns = pl.ds(pl.multiple_of(lax.rem(i, 2) * STEP, STEP), STEP)
        right[...] += lax.dot_general(tgt[lax.div(i, 2), :, columns], own, nt, preferred_element_type=F32)

    pl.semaphore_wait(barrier, len(peers))

    count = [0]
    sent = []

    def copy(src, dst, recv_sem, device, when=None):
        made = remote(src, dst, ssem.at[count[0]], recv_sem, device)
        count[0] += 1
        sent.append((made, when))
        if when is None:
            made.start()
        else:
            pl.when(when)(made.start)

    def wait(ref, sem):
        remote(ref, ref, ssem.at[0], sem, sibling).wait_recv()

    def lanes(block, size=BLOCK):
        return pl.ds(pl.multiple_of(block * size, size), size)

    half, other_half = pl.ds(32 * c, 32), pl.ds(32 * (1 - c), 32)

    rh[b] = right[...]
    for o, peer in zip(bothers, bmates):
        copy(rh.at[b], rh.at[b], hsem.at[b], peer)
    def two_blocks(which, slot, first_d):
        steps = (first_d, first_d + 1)
        for n, d in enumerate(steps):
            row = pl.multiple_of((which * 4 + lax.rem(y + d, 4)) * BLOCK, BLOCK)
            pair[n * BLOCK : (n + 1) * BLOCK, :] = frow[pl.ds(row, BLOCK), :]
        acc[...] = jnp.zeros_like(acc)

        @pl.loop(0, 4 * ROWS // STEP)
        def _(i):
            chunk = pl.ds(pl.multiple_of(i * STEP, STEP), STEP)
            acc[...] += jnp.dot(features(pair[...], cnt[chunk, :]), zcol[chunk, :], preferred_element_type=F32)

        for n, d in enumerate(steps):
            part[slot, d - 1] = acc[n * BLOCK : (n + 1) * BLOCK, :]
            if d < 4:
                copy(part.at[slot, d - 1], ybuf.at[d - 1, slot], ysem.at[3 * slot + d - 1], ymates[d - 1])

    two_blocks(1 - zh, 0, 1)
    for o in bothers:
        wait(rh.at[o], hsem.at[o])
    total = rh[0]
    for o in range(1, 8):
        total = total + rh[o]
    total = total * (1.0 / math.sqrt(TOTAL))
    rj[:, lanes(x)] = total
    for peer in xmates:
        copy(rj.at[:, lanes(x)], rj.at[:, lanes(x)], rsem.at[x], peer)
    for core in (0, 1):

        @pl.when(jnp.logical_and(diag, c == core))
        def _(core=core):
            first[...] = total[32 * core : 32 * core + 32]

    for o, peer in zip(fothers, fmates):
        copy(rj.at[pl.ds(32 * lax.rem(o, 2), 32), lanes(x)], first, psem, peer, diag)
    two_blocks(1 - zh, 0, 3)
    for o in xothers:
        wait(rj.at[:, lanes(o)], rsem.at[o])
    for core in (0, 1):

        @pl.when(c == core)
        def _(core=core):
            vj[0, :, core * WIDTH : (core + 1) * WIDTH] = rj[32 * core : 32 * core + 32, :]

    copy(rj.at[other_half, :], vj.at[0, :, lanes(c, WIDTH)], osem, sibling)
    two_blocks(zh, 1, 1)
    two_blocks(zh, 1, 3)

    def over_y(slot):
        total = part[slot, 3]
        for d in range(3):
            wait(ybuf.at[d, slot], ysem.at[3 * slot + d])
            total = total + ybuf[d, slot]
        return total

    zsend[...] = over_y(0)
    copy(zsend, zrecv, zsem, (((1 - zh) * 4 + y) * 4 + x, j))
    gram[...] = over_y(1)
    wait(vj.at[0, :, lanes(1 - c, WIDTH)], osem)

    @pl.when(jnp.logical_not(diag))
    def _():
        wait(first, psem)

    wait(zrecv, zsem)
    gram[...] = (gram[...] + zrecv[...]) * (1.0 / TOTAL)
    copy(gram, gother, gsem, sibling)

    def multiply(it, wait_gram):
        own = lax.dot_general(vj[it, :, lanes(c, WIDTH)], gram[...], nt, precision=HIGHEST, preferred_element_type=F32)
        if wait_gram:
            wait(gother, gsem)
        fb[it, zl] = own + lax.dot_general(
            vj[it, :, lanes(1 - c, WIDTH)], gother[...], nt, precision=HIGHEST, preferred_element_type=F32
        )
        for peer in zmates:
            copy(fb.at[it, zl], fb.at[it, zl], fsem.at[4 * it + zl], peer)

    def image(it, vector):
        for o in zothers:
            wait(fb.at[it, o], fsem.at[4 * it + o])
        return ((fb[it, 0] + fb[it, 1]) + (fb[it, 2] + fb[it, 3])) + RIDGE * vector

    some = (TARGETS // 2, BLOCK)
    match = lax.broadcasted_iota(jnp.int32, some, 0) == lax.broadcasted_iota(jnp.int32, some, 1)
    sublane = lax.broadcasted_iota(jnp.int32, (8, BLOCK), 0)

    def pack(values):
        tile = jnp.zeros((8, BLOCK), F32)
        for i, value in enumerate(values):
            sums = jnp.where(match, jnp.sum(value, axis=1, keepdims=True), 0.0)
            tile = jnp.where(sublane == i, jnp.sum(sums, axis=0, keepdims=True), tile)
        return tile

    def unpack(tile, i):
        return jnp.sum(jnp.where(match, tile[i : i + 1], 0.0), axis=1, keepdims=True)

    def share(base, mine, mates, tile):
        sums[base + mine] = tile
        for peer in mates:
            copy(sums.at[base + mine], sums.at[base + mine], xsem.at[base + mine], peer)

    def shared(base, others):
        for o in others:
            wait(sums.at[base + o], xsem.at[base + o])
        total = sums[base]
        for i in range(1, len(others) + 1):
            total = total + sums[base + i]
        return total

    multiply(0, True)
    r0 = first[...]
    w1 = image(0, r0)
    w1buf[...] = w1
    place = lax.rem(b, 2) * 4 + x
    for peer in spread_to:
        copy(w1buf, vj.at[1, :, lanes(place)], tsem.at[place], peer)
    share(0, x, xmates, pack([r0 * r0, r0 * w1, w1 * w1]))
    share(4, b, bmates, shared(0, xothers))
    for i in range(8):
        wait(vj.at[1, :, BLOCK * i : BLOCK * (i + 1)], tsem.at[i])
    multiply(1, False)
    tile = shared(4, bothers)
    rr0, curve0, square = (unpack(tile, i) for i in range(3))
    a0 = rr0 / curve0
    mu = square / curve0
    r1 = r0 - a0 * w1
    u = w1 - mu * r0
    piece = fb[1, zl] - (0.25 * (mu - RIDGE)) * w1
    share(12, x, xmates, pack([u * piece, 0.25 * (r1 * u)]))
    share(16, y, ymates, shared(12, xothers))
    share(20, z, rmates, shared(16, yothers))
    image1 = image(1, w1) - mu * w1
    tile = shared(20, rothers)
    tau = unpack(tile, 1) / unpack(tile, 0)
    for core in (0, 1):

        @pl.when(c == core)
        def _(core=core):
            fin[0, 32 * core : 32 * core + 32] = a0 * r0 + tau * u
            fin[1, 32 * core : 32 * core + 32] = r1 - tau * image1

    copy(fin.at[:, half], fin.at[:, half], esem, sibling)
    wait(fin.at[:, other_half], esem)
    sol[...] = fin[0]
    res[...] = fin[1]
    for made, when in sent:
        if when is None:
            made.wait_send()
        else:
            pl.when(when)(made.wait_send)


def solve(counters, targets, frow, fcol, phases):
    vmem = pl.BlockSpec(memory_space=pltpu.VMEM)
    dma = pltpu.SemaphoreType.DMA
    vector, some = (TARGETS, BLOCK), (TARGETS // 2, BLOCK)
    shapes = [
        (2, 4, BLOCK, WIDTH), (3, 2, BLOCK, WIDTH), (BLOCK, WIDTH), (BLOCK, WIDTH), (BLOCK, WIDTH), (8,) + vector, (TARGETS, WIDTH),
        (2, TARGETS // 2, 2 * WIDTH), some, (2, 4) + some, (28, 8, BLOCK), some, (2,) + vector,
    ]
    return pl.pallas_call(
        solve_kernel,
        out_shape=(
            jax.ShapeDtypeStruct(vector, F32),
            jax.ShapeDtypeStruct(vector, F32),
            jax.ShapeDtypeStruct((BLOCK, WIDTH), F32),
        ),
        in_specs=[vmem] * 5,
        out_specs=(vmem,) * 3,
        scratch_shapes=[
            pltpu.VMEM((4 * ROWS, WIDTH), jnp.bfloat16),
            pltpu.VMEM(vector, F32),
            pltpu.VMEM((2 * BLOCK, DEPTH + 128), jnp.bfloat16),
            pltpu.VMEM((2 * BLOCK, WIDTH), F32),
        ]
        + [pltpu.VMEM(shape, F32) for shape in shapes]
        + [
            dma((96,)), dma((8,)), dma((4,)), dma, dma, dma((6,)), dma, dma, dma((8,)), dma((8,)),
            dma((28,)), dma,
        ],
        compiler_params=pltpu.CompilerParams(collective_id=1, has_side_effects=True, vmem_limit_bytes=40 << 20),
        name="solve",
    )(counters.reshape(4 * ROWS, DEPTH), targets, frow, fcol, phases)


def on_device(counters, frequencies, phases, targets):
    columns = jnp.concatenate([frequencies.T, jnp.broadcast_to(phases.T, (WIDTH, 128))], axis=1)
    all_counters, all_targets, rows = gather(counters, targets.T, columns)
    solution, residual, gram = solve(all_counters, all_targets, rows, frequencies, phases)
    return solution.T, residual.T, gram


def solution(mesh):
    return jax.shard_map(
        on_device,
        mesh=mesh,
        in_specs=(P("samp", None), P(None, "feat"), P(None, "feat"), P("samp", None)),
        out_specs=(P("samp", None), P("samp", None), P("samp", "feat")),
        check_vma=False,
    )
```

```python
import math

import jax
import jax.numpy as jnp
from jax import lax
from jax.experimental import pallas as pl
from jax.experimental.pallas import tpu as pltpu
from jax.sharding import PartitionSpec as P

RIDGE = 0.05
ROWS, DEPTH, WIDTH, TARGETS, BLOCK = 1024, 512, 512, 64, 128
TOTAL = 32768
STEP = 512
MESH = pl.DeviceIdType.MESH
SINE = (4.442883014678955, -7.308241367340088, 3.6062889099121094, -0.8457635641098022, 0.10920573770999908)
HIGHEST = lax.Precision.HIGHEST
F32 = jnp.float32


def cosine(angle):
    turns = angle * (0.5 / math.pi)
    f = turns - jnp.round(turns)
    square = f * f
    poly = SINE[-1]
    for coefficient in SINE[-2::-1]:
        poly = poly * square + coefficient
    root = poly * f
    return (1.0 - root * root).astype(jnp.bfloat16)


def remote(src, dst, send_sem, recv_sem, device):
    return pltpu.make_async_remote_copy(
        src_ref=src, dst_ref=dst, send_sem=send_sem, recv_sem=recv_sem, device_id=device, device_id_type=MESH
    )


def greet(peers):
    barrier = pltpu.get_barrier_semaphore()
    for peer in peers:
        pl.semaphore_signal(barrier, inc=1, device_id=peer, device_id_type=MESH)
    pl.semaphore_wait(barrier, len(peers))


def gather_kernel(cnt, tgt, frq, fcol, phase, cg, tg, fr, zcol, ssem, rsem, fsend, frecv, lsem):
    s, j = lax.axis_index("samp"), lax.axis_index("feat")
    x, c, zl, zh = lax.rem(s, 4), lax.rem(j, 2), lax.div(j, 2), lax.div(s, 16)
    z = zh * 4 + zl
    right = (s - x + lax.rem(x + 1, 4), j)
    left = (s - x + lax.rem(x + 3, 4), j)
    sibling = (s, j + 1 - 2 * c)

    def along_z(dz, core):
        other = lax.rem(z + dz + 8, 8)
        return (lax.div(other, 4) * 16 + lax.rem(s, 16), lax.rem(other, 4) * 2 + core)

    far = 2 - 4 * c
    greet(
        [right, left, sibling]
        + [along_z(dz, core) for dz in (1, -1) for core in (0, 1)]
        + [along_z(far, 0), along_z(far, 1), along_z(-far, c)]
    )

    half = STEP * c
    a_rows, b_rows = pl.ds(pl.multiple_of(half, 256), 256), pl.ds(pl.multiple_of(half + 256, 256), 256)
    a_cols = pl.ds(pl.multiple_of(half, 256), 256)
    b_cols = pl.ds(pl.multiple_of(half + 256, 256), 256)

    def pair(i, src_c, src_t, slot, part, device):
        rows, cols = (a_rows, a_cols) if part == 0 else (b_rows, b_cols)
        return [
            remote(src_c.at[rows], cg.at[slot, rows], ssem.at[2 * i], rsem.at[2 * i], device),
            remote(src_t.at[:, cols], tg.at[slot, :, cols], ssem.at[2 * i + 1], rsem.at[2 * i + 1], device),
        ]

    def twin(i, slot, part):
        other = STEP - half
        rows = pl.ds(pl.multiple_of(other + 256 * part, 256), 256)
        cols = pl.ds(pl.multiple_of(other + 256 * part, 256), 256)
        return [
            remote(cg.at[slot, rows], cg.at[slot, rows], ssem.at[2 * i], rsem.at[2 * i], sibling),
            remote(tg.at[slot, :, cols], tg.at[slot, :, cols], ssem.at[2 * i + 1], rsem.at[2 * i + 1], sibling),
        ]

    to_right = [pair(0, cnt, tgt, 1, 0, right), pair(1, cnt, tgt, 1, 1, right)]
    to_left = [pair(2, cnt, tgt, 2, 0, left), pair(3, cnt, tgt, 2, 1, left)]
    on_right = pair(4, cg.at[1], tg.at[1], 3, 0, right)
    on_left = pair(5, cg.at[2], tg.at[2], 3, 1, left)
    across = {
        (slot, part): pair(6 + 2 * (slot - 1) + part, cg.at[slot], tg.at[slot], slot, part, sibling)
        for slot in (1, 2, 3)
        for part in (0, 1)
    }

    def go(copies):
        for copy in copies:
            copy.start()

    def got(copies):
        for copy in copies:
            copy.wait_recv()

    go(to_right[0])
    go(to_left[1])
    quarter = pl.ds(pl.multiple_of(BLOCK * x, BLOCK), BLOCK)
    mine = pl.ds(pl.multiple_of(BLOCK * j, BLOCK), BLOCK)
    spread = []
    for i, (dz, core) in enumerate([(1, 0), (1, 1), (-1, 0), (-1, 1), (far, 0), (far, 1)]):
        spread.append(remote(frq.at[quarter], fr.at[mine], fsend.at[i], frecv.at[2 * (i // 2) + c], along_z(dz, core)))
    spread.append(remote(frq.at[quarter], fr.at[mine], fsend.at[6], frecv.at[6], sibling))
    go(spread)
    go(to_right[1])
    go(to_left[0])
    local = [
        pltpu.make_async_copy(cnt, cg.at[0], lsem.at[0]),
        pltpu.make_async_copy(tgt, tg.at[0], lsem.at[1]),
        pltpu.make_async_copy(frq.at[quarter], fr.at[mine], lsem.at[2]),
    ]
    go(local)
    def columns(slot, rows):
        mixed = jnp.dot(cg[slot, rows, :], fcol[...], preferred_element_type=F32)
        zcol[slot, rows, :] = cosine(mixed + phase[...].astype(F32))

    here, there = pl.ds(pl.multiple_of(half, STEP), STEP), pl.ds(pl.multiple_of(STEP - half, STEP), STEP)
    local[0].wait()
    columns(0, here)
    got(to_right[0])
    go(on_right)
    go(across[1, 0])
    got(to_left[1])
    go(on_left)
    go(across[2, 1])
    columns(0, there)
    got(to_right[1])
    go(across[1, 1])
    got(to_left[0])
    go(across[2, 0])
    columns(1, here)
    columns(2, here)
    got(on_right)
    go(across[3, 0])
    got(on_left)
    go(across[3, 1])
    for slot in (1, 2, 3):
        if slot == 3:
            columns(3, here)
        for part in (0, 1):
            got(twin(6 + 2 * (slot - 1) + part, slot, part))
        columns(slot, there)
    for i, (dz, core) in enumerate([(-1, 0), (-1, 1), (1, 0), (1, 1), (-2, 0), (2, 1)]):
        source = along_z(dz, core)
        rows = pl.ds(pl.multiple_of(BLOCK * source[1], BLOCK), BLOCK)
        remote(frq.at[quarter], fr.at[rows], fsend.at[i], frecv.at[2 * (i // 2) + core], source).wait_recv()
    rows = pl.ds(pl.multiple_of(BLOCK * sibling[1], BLOCK), BLOCK)
    remote(frq.at[quarter], fr.at[rows], fsend.at[6], frecv.at[6], sibling).wait_recv()
    for copy in local[1:]:
        copy.wait()
    sent = to_right[0] + to_right[1] + to_left[0] + to_left[1] + on_right + on_left + spread
    for copies in across.values():
        sent = sent + copies
    for copy in sent:
        copy.wait_send()


def gather(counters, targets, frequencies, columns, phases):
    bf16 = jnp.bfloat16
    vmem = pl.BlockSpec(memory_space=pltpu.VMEM)
    return pl.pallas_call(
        gather_kernel,
        out_shape=(
            jax.ShapeDtypeStruct((4, ROWS, DEPTH), bf16),
            jax.ShapeDtypeStruct((4, TARGETS, ROWS), bf16),
            jax.ShapeDtypeStruct((8 * BLOCK, DEPTH + 128), bf16),
            jax.ShapeDtypeStruct((4, ROWS, WIDTH), bf16),
        ),
        in_specs=[vmem] * 5,
        out_specs=(vmem,) * 4,
        scratch_shapes=[
            pltpu.SemaphoreType.DMA((24,)),
            pltpu.SemaphoreType.DMA((24,)),
            pltpu.SemaphoreType.DMA((7,)),
            pltpu.SemaphoreType.DMA((7,)),
            pltpu.SemaphoreType.DMA((3,)),
        ],
        compiler_params=pltpu.CompilerParams(collective_id=0, has_side_effects=True, vmem_limit_bytes=32 << 20),
        name="gather",
    )(counters, targets, frequencies, columns, phases)


def solve_kernel(
    cnt, tgt, frow, zcol, sol, res, gram,
    right, pair, acc, part, ybuf, zsend, zrecv, gother, rh, rj, vj, first, fb, sums, w1buf, fin,
    ssem, hsem, rsem, osem, psem, ysem, zsem, gsem, fsem, tsem, xsem, esem,
):
    s, j = lax.axis_index("samp"), lax.axis_index("feat")
    x, b = lax.rem(s, 4), lax.div(s, 4)
    y, zh = lax.rem(b, 4), lax.div(b, 4)
    c, zl = lax.rem(j, 2), lax.div(j, 2)
    diag = b == j
    sibling = (s, j + 1 - 2 * c)
    xothers = [lax.rem(x + d, 4) for d in (1, 2, 3)]
    xmates = [(b * 4 + o, j) for o in xothers]
    bothers = [lax.rem(b + e, 8) for e in range(1, 8)]
    bmates = [(o * 4 + x, j) for o in bothers]
    fothers = [lax.rem(j + e, 8) for e in range(1, 8)]
    fmates = [(s, o) for o in fothers]
    zothers = [lax.rem(zl + d, 4) for d in (1, 2, 3)]
    zmates = [(s, o * 2 + c) for o in zothers]
    yothers = [lax.rem(y + d, 4) for d in (1, 2, 3)]
    ymates = [((zh * 4 + o) * 4 + x, j) for o in yothers]
    z = zh * 4 + zl
    rothers = [lax.rem(z + e, 8) for e in range(1, 8)]
    rmates = [((lax.div(o, 4) * 4 + y) * 4 + x, lax.rem(o, 4) * 2 + c) for o in rothers]
    across = [((1 - zh) * 16 + y * 4 + x, o * 2 + c) for o in zothers]
    down = lax.div(b, 2)
    same = lax.div(zl, 2) == zh
    near = jnp.where(same, zl == down, zl == 3 * (1 - zh))
    to_zh = jnp.where(same, zh, 1 - zh)
    skip = jnp.where(near, 2, 0)
    spread_to = [((to_zh * 4 + lax.rem(y + skip + d, 4)) * 4 + o, down * 2 + c) for d in (0, 1) for o in range(4)]
    spread_from = []
    for h in (0, 1):
        source_y, source_zh = lax.rem(zl, 2) * 2 + h, lax.div(zl, 2)
        far = jnp.where(lax.rem(y + 4 - source_y, 4) < 2, 1, 0)
        inside = zl + far * (1 - 2 * lax.rem(zl, 2))
        outside = jnp.where(source_zh == 0, 3 - far, far)
        source_zl = jnp.where(zh == source_zh, inside, outside)
        spread_from += [((zl * 2 + h) * 4 + o, source_zl * 2 + c) for o in range(4)]

    barrier = pltpu.get_barrier_semaphore()
    peers = xmates + bmates + fmates + across + spread_from
    for peer in peers:
        pl.semaphore_signal(barrier, inc=1, device_id=peer, device_id_type=MESH)

    count = [0]
    sent = []

    def copy(src, dst, recv_sem, device, when=None):
        made = remote(src, dst, ssem.at[count[0]], recv_sem, device)
        count[0] += 1
        sent.append((made, when))
        if when is None:
            made.start()
        else:
            pl.when(when)(made.start)

    def wait(ref, sem):
        remote(ref, ref, ssem.at[0], sem, sibling).wait_recv()

    def lanes(block, size=BLOCK):
        return pl.ds(pl.multiple_of(block * size, size), size)

    half, other_half = pl.ds(32 * c, 32), pl.ds(32 * (1 - c), 32)

    nt = (((1,), (1,)), ((), ()))

    def features(block, rows):
        mixed = lax.dot_general(block[:, :DEPTH], rows, nt, preferred_element_type=F32)
        return cosine(mixed + block[:, DEPTH : DEPTH + 1].astype(F32))

    def two_blocks(which, slot, first_d):
        steps = (first_d, first_d + 1)
        for n, d in enumerate(steps):
            row = pl.multiple_of((which * 4 + lax.rem(y + d, 4)) * BLOCK, BLOCK)
            pair[n * BLOCK : (n + 1) * BLOCK, :] = frow[pl.ds(row, BLOCK), :]
        acc[...] = jnp.zeros_like(acc)

        @pl.loop(0, 4 * ROWS // STEP)
        def _(i):
            chunk = pl.ds(pl.multiple_of(i * STEP, STEP), STEP)
            acc[...] += jnp.dot(features(pair[...], cnt[chunk, :]), zcol[chunk, :], preferred_element_type=F32)

        if (slot, first_d) == (0, 1):
            pl.semaphore_wait(barrier, len(peers))
        for n, d in enumerate(steps):
            part[slot, d - 1] = acc[n * BLOCK : (n + 1) * BLOCK, :]
            if d < 4:
                copy(part.at[slot, d - 1], ybuf.at[d - 1, slot], ysem.at[3 * slot + d - 1], ymates[d - 1])

    two_blocks(1 - zh, 0, 1)
    right[...] = jnp.zeros_like(right)

    @pl.loop(0, 4 * ROWS // STEP)
    def _(i):
        own = features(
            frow[pl.ds(pl.multiple_of(BLOCK * j, BLOCK), BLOCK), :],
            cnt[pl.ds(pl.multiple_of(i * STEP, STEP), STEP), :],
        )
        columns = pl.ds(pl.multiple_of(lax.rem(i, 2) * STEP, STEP), STEP)
        right[...] += lax.dot_general(tgt[lax.div(i, 2), :, columns], own, nt, preferred_element_type=F32)

    rh[b] = right[...]
    for o, peer in zip(bothers, bmates):
        copy(rh.at[b], rh.at[b], hsem.at[b], peer)
    two_blocks(1 - zh, 0, 3)
    for o in bothers:
        wait(rh.at[o], hsem.at[o])
    total = rh[0]
    for o in range(1, 8):
        total = total + rh[o]
    total = total * (1.0 / math.sqrt(TOTAL))
    rj[:, lanes(x)] = total
    for peer in xmates:
        copy(rj.at[:, lanes(x)], rj.at[:, lanes(x)], rsem.at[x], peer)
    for core in (0, 1):

        @pl.when(jnp.logical_and(diag, c == core))
        def _(core=core):
            first[...] = total[32 * core : 32 * core + 32]

    for o, peer in zip(fothers, fmates):
        copy(rj.at[pl.ds(32 * lax.rem(o, 2), 32), lanes(x)], first, psem, peer, diag)
    two_blocks(zh, 1, 1)

    def over_y(slot):
        total = part[slot, 3]
        for d in range(3):
            wait(ybuf.at[d, slot], ysem.at[3 * slot + d])
            total = total + ybuf[d, slot]
        return total

    zsend[...] = over_y(0)
    copy(zsend, zrecv, zsem, (((1 - zh) * 4 + y) * 4 + x, j))
    two_blocks(zh, 1, 3)
    for o in xothers:
        wait(rj.at[:, lanes(o)], rsem.at[o])
    for core in (0, 1):

        @pl.when(c == core)
        def _(core=core):
            vj[0, :, core * WIDTH : (core + 1) * WIDTH] = rj[32 * core : 32 * core + 32, :]

    copy(rj.at[other_half, :], vj.at[0, :, lanes(c, WIDTH)], osem, sibling)
    gram[...] = over_y(1)
    wait(vj.at[0, :, lanes(1 - c, WIDTH)], osem)

    @pl.when(jnp.logical_not(diag))
    def _():
        wait(first, psem)

    wait(zrecv, zsem)
    gram[...] = (gram[...] + zrecv[...]) * (1.0 / TOTAL)
    copy(gram, gother, gsem, sibling)

    def multiply(it, wait_gram):
        own = lax.dot_general(vj[it, :, lanes(c, WIDTH)], gram[...], nt, precision=HIGHEST, preferred_element_type=F32)
        if wait_gram:
            wait(gother, gsem)
        fb[it, zl] = own + lax.dot_general(
            vj[it, :, lanes(1 - c, WIDTH)], gother[...], nt, precision=HIGHEST, preferred_element_type=F32
        )
        for peer in zmates:
            copy(fb.at[it, zl], fb.at[it, zl], fsem.at[4 * it + zl], peer)

    def image(it, vector):
        for o in zothers:
            wait(fb.at[it, o], fsem.at[4 * it + o])
        return ((fb[it, 0] + fb[it, 1]) + (fb[it, 2] + fb[it, 3])) + RIDGE * vector

    some = (TARGETS // 2, BLOCK)
    match = lax.broadcasted_iota(jnp.int32, some, 0) == lax.broadcasted_iota(jnp.int32, some, 1)
    sublane = lax.broadcasted_iota(jnp.int32, (8, BLOCK), 0)

    def pack(values):
        tile = jnp.zeros((8, BLOCK), F32)
        for i, value in enumerate(values):
            sums = jnp.where(match, jnp.sum(value, axis=1, keepdims=True), 0.0)
            tile = jnp.where(sublane == i, jnp.sum(sums, axis=0, keepdims=True), tile)
        return tile

    def unpack(tile, i):
        return jnp.sum(jnp.where(match, tile[i : i + 1], 0.0), axis=1, keepdims=True)

    def share(base, mine, mates, tile):
        sums[base + mine] = tile
        for peer in mates:
            copy(sums.at[base + mine], sums.at[base + mine], xsem.at[base + mine], peer)

    def shared(base, others):
        for o in others:
            wait(sums.at[base + o], xsem.at[base + o])
        total = sums[base]
        for i in range(1, len(others) + 1):
            total = total + sums[base + i]
        return total

    multiply(0, True)
    r0 = first[...]
    w1 = image(0, r0)
    w1buf[...] = w1
    place = lax.rem(b, 2) * 4 + x
    for peer in spread_to:
        copy(w1buf, vj.at[1, :, lanes(place)], tsem.at[place], peer)
    share(0, x, xmates, pack([r0 * r0, r0 * w1, w1 * w1]))
    share(4, b, bmates, shared(0, xothers))
    for i in range(8):
        wait(vj.at[1, :, BLOCK * i : BLOCK * (i + 1)], tsem.at[i])
    multiply(1, False)
    tile = shared(4, bothers)
    rr0, curve0, square = (unpack(tile, i) for i in range(3))
    a0 = rr0 / curve0
    mu = square / curve0
    r1 = r0 - a0 * w1
    u = w1 - mu * r0
    piece = fb[1, zl] - (0.25 * (mu - RIDGE)) * w1
    share(12, x, xmates, pack([u * piece, 0.25 * (r1 * u)]))
    share(16, y, ymates, shared(12, xothers))
    share(20, z, rmates, shared(16, yothers))
    image1 = image(1, w1) - mu * w1
    tile = shared(20, rothers)
    tau = unpack(tile, 1) / unpack(tile, 0)
    for core in (0, 1):

        @pl.when(c == core)
        def _(core=core):
            fin[0, 32 * core : 32 * core + 32] = a0 * r0 + tau * u
            fin[1, 32 * core : 32 * core + 32] = r1 - tau * image1

    copy(fin.at[:, half], fin.at[:, half], esem, sibling)
    wait(fin.at[:, other_half], esem)
    sol[...] = fin[0]
    res[...] = fin[1]
    for made, when in sent:
        if when is None:
            made.wait_send()
        else:
            pl.when(when)(made.wait_send)


def solve(counters, targets, frow, zcol):
    vmem = pl.BlockSpec(memory_space=pltpu.VMEM)
    dma = pltpu.SemaphoreType.DMA
    vector, some = (TARGETS, BLOCK), (TARGETS // 2, BLOCK)
    shapes = [
        (2, 4, BLOCK, WIDTH), (3, 2, BLOCK, WIDTH), (BLOCK, WIDTH), (BLOCK, WIDTH), (BLOCK, WIDTH), (8,) + vector, (TARGETS, WIDTH),
        (2, TARGETS // 2, 2 * WIDTH), some, (2, 4) + some, (28, 8, BLOCK), some, (2,) + vector,
    ]
    return pl.pallas_call(
        solve_kernel,
        out_shape=(
            jax.ShapeDtypeStruct(vector, F32),
            jax.ShapeDtypeStruct(vector, F32),
            jax.ShapeDtypeStruct((BLOCK, WIDTH), F32),
        ),
        in_specs=[vmem] * 4,
        out_specs=(vmem,) * 3,
        scratch_shapes=[
            pltpu.VMEM(vector, F32),
            pltpu.VMEM((2 * BLOCK, DEPTH + 128), jnp.bfloat16),
            pltpu.VMEM((2 * BLOCK, WIDTH), F32),
        ]
        + [pltpu.VMEM(shape, F32) for shape in shapes]
        + [
            dma((96,)), dma((8,)), dma((4,)), dma, dma, dma((6,)), dma, dma, dma((8,)), dma((8,)),
            dma((28,)), dma,
        ],
        compiler_params=pltpu.CompilerParams(collective_id=1, has_side_effects=True, vmem_limit_bytes=40 << 20),
        name="solve",
    )(counters.reshape(4 * ROWS, DEPTH), targets, frow, zcol.reshape(4 * ROWS, WIDTH))


def on_device(counters, frequencies, phases, targets):
    columns = jnp.concatenate([frequencies.T, jnp.broadcast_to(phases.T, (WIDTH, 128))], axis=1)
    solution, residual, gram = solve(*gather(counters, targets.T, columns, frequencies, phases))
    return solution.T, residual.T, gram


def solution(mesh):
    return jax.shard_map(
        on_device,
        mesh=mesh,
        in_specs=(P("samp", None), P(None, "feat"), P(None, "feat"), P("samp", None)),
        out_specs=(P("samp", None), P("samp", None), P("samp", "feat")),
        check_vma=False,
    )
```

```python
import math

import jax
import jax.numpy as jnp
from jax import lax
from jax.experimental import pallas as pl
from jax.experimental.pallas import tpu as pltpu
from jax.sharding import PartitionSpec as P

RIDGE = 0.05
ROWS, DEPTH, WIDTH, TARGETS, BLOCK = 1024, 512, 512, 64, 128
TOTAL = 32768
STEP = 512
MESH = pl.DeviceIdType.MESH
SINE = (4.442883014678955, -7.308241367340088, 3.6062889099121094, -0.8457635641098022, 0.10920573770999908)
HIGHEST = lax.Precision.HIGHEST
F32 = jnp.float32


def cosine(angle):
    turns = angle * (0.5 / math.pi)
    f = turns - jnp.round(turns)
    square = f * f
    poly = SINE[-1]
    for coefficient in SINE[-2::-1]:
        poly = poly * square + coefficient
    root = poly * f
    return (1.0 - root * root).astype(jnp.bfloat16)


NT = (((1,), (1,)), ((), ()))


def features(block, rows):
    mixed = lax.dot_general(block[:, :DEPTH], rows, NT, preferred_element_type=F32)
    return cosine(mixed + block[:, DEPTH : DEPTH + 1].astype(F32))


def remote(src, dst, send_sem, recv_sem, device):
    return pltpu.make_async_remote_copy(
        src_ref=src, dst_ref=dst, send_sem=send_sem, recv_sem=recv_sem, device_id=device, device_id_type=MESH
    )


def greet(peers):
    barrier = pltpu.get_barrier_semaphore()
    for peer in peers:
        pl.semaphore_signal(barrier, inc=1, device_id=peer, device_id_type=MESH)
    pl.semaphore_wait(barrier, len(peers))


def gather_kernel(cnt, tgt, frq, fcol, phase, cg, tg, fr, zcol, rpart, ssem, rsem, fsend, frecv, lsem):
    s, j = lax.axis_index("samp"), lax.axis_index("feat")
    x, c, zl, zh = lax.rem(s, 4), lax.rem(j, 2), lax.div(j, 2), lax.div(s, 16)
    z = zh * 4 + zl
    right = (s - x + lax.rem(x + 1, 4), j)
    left = (s - x + lax.rem(x + 3, 4), j)
    sibling = (s, j + 1 - 2 * c)

    def along_z(dz, core):
        other = lax.rem(z + dz + 8, 8)
        return (lax.div(other, 4) * 16 + lax.rem(s, 16), lax.rem(other, 4) * 2 + core)

    far = 2 - 4 * c
    greet(
        [right, left, sibling]
        + [along_z(dz, core) for dz in (1, -1) for core in (0, 1)]
        + [along_z(far, 0), along_z(far, 1), along_z(-far, c)]
    )

    half = STEP * c
    a_rows, b_rows = pl.ds(pl.multiple_of(half, 256), 256), pl.ds(pl.multiple_of(half + 256, 256), 256)
    a_cols = pl.ds(pl.multiple_of(half, 256), 256)
    b_cols = pl.ds(pl.multiple_of(half + 256, 256), 256)

    def pair(i, src_c, src_t, slot, part, device):
        rows, cols = (a_rows, a_cols) if part == 0 else (b_rows, b_cols)
        return [
            remote(src_c.at[rows], cg.at[slot, rows], ssem.at[2 * i], rsem.at[2 * i], device),
            remote(src_t.at[:, cols], tg.at[slot, :, cols], ssem.at[2 * i + 1], rsem.at[2 * i + 1], device),
        ]

    def twin(i, slot, part):
        other = STEP - half
        rows = pl.ds(pl.multiple_of(other + 256 * part, 256), 256)
        cols = pl.ds(pl.multiple_of(other + 256 * part, 256), 256)
        return [
            remote(cg.at[slot, rows], cg.at[slot, rows], ssem.at[2 * i], rsem.at[2 * i], sibling),
            remote(tg.at[slot, :, cols], tg.at[slot, :, cols], ssem.at[2 * i + 1], rsem.at[2 * i + 1], sibling),
        ]

    to_right = [pair(0, cnt, tgt, 1, 0, right), pair(1, cnt, tgt, 1, 1, right)]
    to_left = [pair(2, cnt, tgt, 2, 0, left), pair(3, cnt, tgt, 2, 1, left)]
    on_right = pair(4, cg.at[1], tg.at[1], 3, 0, right)
    on_left = pair(5, cg.at[2], tg.at[2], 3, 1, left)
    across = {
        (slot, part): pair(6 + 2 * (slot - 1) + part, cg.at[slot], tg.at[slot], slot, part, sibling)
        for slot in (1, 2, 3)
        for part in (0, 1)
    }

    def go(copies):
        for copy in copies:
            copy.start()

    def got(copies):
        for copy in copies:
            copy.wait_recv()

    go(to_right[0])
    go(to_left[1])
    quarter = pl.ds(pl.multiple_of(BLOCK * x, BLOCK), BLOCK)
    mine = pl.ds(pl.multiple_of(BLOCK * j, BLOCK), BLOCK)
    spread = []
    for i, (dz, core) in enumerate([(1, 0), (1, 1), (-1, 0), (-1, 1), (far, 0), (far, 1)]):
        spread.append(remote(frq.at[quarter], fr.at[mine], fsend.at[i], frecv.at[2 * (i // 2) + c], along_z(dz, core)))
    spread.append(remote(frq.at[quarter], fr.at[mine], fsend.at[6], frecv.at[6], sibling))
    go(spread)
    go(to_right[1])
    go(to_left[0])
    local = [
        pltpu.make_async_copy(cnt, cg.at[0], lsem.at[0]),
        pltpu.make_async_copy(tgt, tg.at[0], lsem.at[1]),
        pltpu.make_async_copy(frq.at[quarter], fr.at[mine], lsem.at[2]),
    ]
    go(local)
    def columns(slot, rows):
        mixed = jnp.dot(cg[slot, rows, :], fcol[...], preferred_element_type=F32)
        zcol[slot, rows, :] = cosine(mixed + phase[...].astype(F32))
        samples = pl.ds(pl.multiple_of(rows.start, STEP), STEP)
        own = features(frq[quarter, :], cg[slot, rows, :])
        rpart[...] += lax.dot_general(tg[slot, :, samples], own, NT, preferred_element_type=F32)

    here, there = pl.ds(pl.multiple_of(half, STEP), STEP), pl.ds(pl.multiple_of(STEP - half, STEP), STEP)
    rpart[...] = jnp.zeros_like(rpart)
    local[0].wait()
    local[1].wait()
    columns(0, here)
    got(to_right[0])
    go(on_right)
    go(across[1, 0])
    got(to_left[1])
    go(on_left)
    go(across[2, 1])
    columns(0, there)
    got(to_right[1])
    go(across[1, 1])
    got(to_left[0])
    go(across[2, 0])
    columns(1, here)
    columns(2, here)
    got(on_right)
    go(across[3, 0])
    got(on_left)
    go(across[3, 1])
    for slot in (1, 2, 3):
        if slot == 3:
            columns(3, here)
        for part in (0, 1):
            got(twin(6 + 2 * (slot - 1) + part, slot, part))
        columns(slot, there)
    for i, (dz, core) in enumerate([(-1, 0), (-1, 1), (1, 0), (1, 1), (-2, 0), (2, 1)]):
        source = along_z(dz, core)
        rows = pl.ds(pl.multiple_of(BLOCK * source[1], BLOCK), BLOCK)
        remote(frq.at[quarter], fr.at[rows], fsend.at[i], frecv.at[2 * (i // 2) + core], source).wait_recv()
    rows = pl.ds(pl.multiple_of(BLOCK * sibling[1], BLOCK), BLOCK)
    remote(frq.at[quarter], fr.at[rows], fsend.at[6], frecv.at[6], sibling).wait_recv()
    local[2].wait()
    sent = to_right[0] + to_right[1] + to_left[0] + to_left[1] + on_right + on_left + spread
    for copies in across.values():
        sent = sent + copies
    for copy in sent:
        copy.wait_send()


def gather(counters, targets, frequencies, columns, phases):
    bf16 = jnp.bfloat16
    vmem = pl.BlockSpec(memory_space=pltpu.VMEM)
    return pl.pallas_call(
        gather_kernel,
        out_shape=(
            jax.ShapeDtypeStruct((4, ROWS, DEPTH), bf16),
            jax.ShapeDtypeStruct((4, TARGETS, ROWS), bf16),
            jax.ShapeDtypeStruct((8 * BLOCK, DEPTH + 128), bf16),
            jax.ShapeDtypeStruct((4, ROWS, WIDTH), bf16),
            jax.ShapeDtypeStruct((TARGETS, BLOCK), F32),
        ),
        in_specs=[vmem] * 5,
        out_specs=(vmem,) * 5,
        scratch_shapes=[
            pltpu.SemaphoreType.DMA((24,)),
            pltpu.SemaphoreType.DMA((24,)),
            pltpu.SemaphoreType.DMA((7,)),
            pltpu.SemaphoreType.DMA((7,)),
            pltpu.SemaphoreType.DMA((3,)),
        ],
        compiler_params=pltpu.CompilerParams(collective_id=0, has_side_effects=True, vmem_limit_bytes=32 << 20),
        name="gather",
    )(counters, targets, frequencies, columns, phases)


def solve_kernel(
    cnt, frow, zcol, right, sol, res, gram,
    pair, acc, part, ybuf, zsend, zrecv, gother, rh, rj, vj, first, fb, sums, w1buf, fin,
    ssem, hsem, rsem, osem, psem, ysem, zsem, gsem, fsem, tsem, xsem, esem,
):
    s, j = lax.axis_index("samp"), lax.axis_index("feat")
    x, b = lax.rem(s, 4), lax.div(s, 4)
    y, zh = lax.rem(b, 4), lax.div(b, 4)
    c, zl = lax.rem(j, 2), lax.div(j, 2)
    diag = b == j
    sibling = (s, j + 1 - 2 * c)
    xothers = [lax.rem(x + d, 4) for d in (1, 2, 3)]
    xmates = [(b * 4 + o, j) for o in xothers]
    bothers = [lax.rem(b + e, 8) for e in range(1, 8)]
    bmates = [(o * 4 + x, j) for o in bothers]
    fothers = [lax.rem(j + e, 8) for e in range(1, 8)]
    fmates = [(s, o) for o in fothers]
    zothers = [lax.rem(zl + d, 4) for d in (1, 2, 3)]
    zmates = [(s, o * 2 + c) for o in zothers]
    yothers = [lax.rem(y + d, 4) for d in (1, 2, 3)]
    ymates = [((zh * 4 + o) * 4 + x, j) for o in yothers]
    z = zh * 4 + zl
    rothers = [lax.rem(z + e, 8) for e in range(1, 8)]
    rmates = [((lax.div(o, 4) * 4 + y) * 4 + x, lax.rem(o, 4) * 2 + c) for o in rothers]
    across = [((1 - zh) * 16 + y * 4 + x, o * 2 + c) for o in zothers]
    down = lax.div(b, 2)
    same = lax.div(zl, 2) == zh
    near = jnp.where(same, zl == down, zl == 3 * (1 - zh))
    to_zh = jnp.where(same, zh, 1 - zh)
    skip = jnp.where(near, 2, 0)
    spread_to = [((to_zh * 4 + lax.rem(y + skip + d, 4)) * 4 + o, down * 2 + c) for d in (0, 1) for o in range(4)]
    spread_from = []
    for h in (0, 1):
        source_y, source_zh = lax.rem(zl, 2) * 2 + h, lax.div(zl, 2)
        far = jnp.where(lax.rem(y + 4 - source_y, 4) < 2, 1, 0)
        inside = zl + far * (1 - 2 * lax.rem(zl, 2))
        outside = jnp.where(source_zh == 0, 3 - far, far)
        source_zl = jnp.where(zh == source_zh, inside, outside)
        spread_from += [((zl * 2 + h) * 4 + o, source_zl * 2 + c) for o in range(4)]

    barrier = pltpu.get_barrier_semaphore()
    peers = xmates + bmates + fmates + across + spread_from
    for peer in peers:
        pl.semaphore_signal(barrier, inc=1, device_id=peer, device_id_type=MESH)

    count = [0]
    sent = []

    def copy(src, dst, recv_sem, device, when=None):
        made = remote(src, dst, ssem.at[count[0]], recv_sem, device)
        count[0] += 1
        sent.append((made, when))
        if when is None:
            made.start()
        else:
            pl.when(when)(made.start)

    def wait(ref, sem):
        remote(ref, ref, ssem.at[0], sem, sibling).wait_recv()

    def lanes(block, size=BLOCK):
        return pl.ds(pl.multiple_of(block * size, size), size)

    half, other_half = pl.ds(32 * c, 32), pl.ds(32 * (1 - c), 32)

    def two_blocks(which, slot, first_d):
        steps = (first_d, first_d + 1)
        for n, d in enumerate(steps):
            row = pl.multiple_of((which * 4 + lax.rem(y + d, 4)) * BLOCK, BLOCK)
            pair[n * BLOCK : (n + 1) * BLOCK, :] = frow[pl.ds(row, BLOCK), :]
        acc[...] = jnp.zeros_like(acc)

        @pl.loop(0, 4 * ROWS // STEP)
        def _(i):
            chunk = pl.ds(pl.multiple_of(i * STEP, STEP), STEP)
            acc[...] += jnp.dot(features(pair[...], cnt[chunk, :]), zcol[chunk, :], preferred_element_type=F32)

        if (slot, first_d) == (0, 1):
            pl.semaphore_wait(barrier, len(peers))
            for peer in bmates:
                copy(right, rh.at[b], hsem.at[b], peer)
        for n, d in enumerate(steps):
            part[slot, d - 1] = acc[n * BLOCK : (n + 1) * BLOCK, :]
            if d < 4:
                copy(part.at[slot, d - 1], ybuf.at[d - 1, slot], ysem.at[3 * slot + d - 1], ymates[d - 1])

    two_blocks(1 - zh, 0, 1)
    two_blocks(1 - zh, 0, 3)
    two_blocks(zh, 1, 1)
    rh[b] = right[...]
    for o in bothers:
        wait(rh.at[o], hsem.at[o])
    total = rh[0]
    for o in range(1, 8):
        total = total + rh[o]
    total = total * (1.0 / math.sqrt(TOTAL))
    rj[:, lanes(x)] = total
    for peer in xmates:
        copy(rj.at[:, lanes(x)], rj.at[:, lanes(x)], rsem.at[x], peer)
    for core in (0, 1):

        @pl.when(jnp.logical_and(diag, c == core))
        def _(core=core):
            first[...] = total[32 * core : 32 * core + 32]

    for o, peer in zip(fothers, fmates):
        copy(rj.at[pl.ds(32 * lax.rem(o, 2), 32), lanes(x)], first, psem, peer, diag)

    def over_y(slot):
        total = part[slot, 3]
        for d in range(3):
            wait(ybuf.at[d, slot], ysem.at[3 * slot + d])
            total = total + ybuf[d, slot]
        return total

    zsend[...] = over_y(0)
    copy(zsend, zrecv, zsem, (((1 - zh) * 4 + y) * 4 + x, j))
    two_blocks(zh, 1, 3)
    for o in xothers:
        wait(rj.at[:, lanes(o)], rsem.at[o])
    for core in (0, 1):

        @pl.when(c == core)
        def _(core=core):
            vj[0, :, core * WIDTH : (core + 1) * WIDTH] = rj[32 * core : 32 * core + 32, :]

    copy(rj.at[other_half, :], vj.at[0, :, lanes(c, WIDTH)], osem, sibling)
    gram[...] = over_y(1)
    wait(vj.at[0, :, lanes(1 - c, WIDTH)], osem)

    @pl.when(jnp.logical_not(diag))
    def _():
        wait(first, psem)

    wait(zrecv, zsem)
    gram[...] = (gram[...] + zrecv[...]) * (1.0 / TOTAL)
    copy(gram, gother, gsem, sibling)

    def multiply(it, wait_gram):
        own = lax.dot_general(vj[it, :, lanes(c, WIDTH)], gram[...], NT, precision=HIGHEST, preferred_element_type=F32)
        if wait_gram:
            wait(gother, gsem)
        fb[it, zl] = own + lax.dot_general(
            vj[it, :, lanes(1 - c, WIDTH)], gother[...], NT, precision=HIGHEST, preferred_element_type=F32
        )
        for peer in zmates:
            copy(fb.at[it, zl], fb.at[it, zl], fsem.at[4 * it + zl], peer)

    def image(it, vector):
        for o in zothers:
            wait(fb.at[it, o], fsem.at[4 * it + o])
        return ((fb[it, 0] + fb[it, 1]) + (fb[it, 2] + fb[it, 3])) + RIDGE * vector

    some = (TARGETS // 2, BLOCK)
    match = lax.broadcasted_iota(jnp.int32, some, 0) == lax.broadcasted_iota(jnp.int32, some, 1)
    sublane = lax.broadcasted_iota(jnp.int32, (8, BLOCK), 0)

    def pack(values):
        tile = jnp.zeros((8, BLOCK), F32)
        for i, value in enumerate(values):
            sums = jnp.where(match, jnp.sum(value, axis=1, keepdims=True), 0.0)
            tile = jnp.where(sublane == i, jnp.sum(sums, axis=0, keepdims=True), tile)
        return tile

    def unpack(tile, i):
        return jnp.sum(jnp.where(match, tile[i : i + 1], 0.0), axis=1, keepdims=True)

    def share(base, mine, mates, tile):
        sums[base + mine] = tile
        for peer in mates:
            copy(sums.at[base + mine], sums.at[base + mine], xsem.at[base + mine], peer)

    def shared(base, others):
        for o in others:
            wait(sums.at[base + o], xsem.at[base + o])
        total = sums[base]
        for i in range(1, len(others) + 1):
            total = total + sums[base + i]
        return total

    multiply(0, True)
    r0 = first[...]
    w1 = image(0, r0)
    w1buf[...] = w1
    place = lax.rem(b, 2) * 4 + x
    for peer in spread_to:
        copy(w1buf, vj.at[1, :, lanes(place)], tsem.at[place], peer)
    share(0, x, xmates, pack([r0 * r0, r0 * w1, w1 * w1]))
    share(4, b, bmates, shared(0, xothers))
    for i in range(8):
        wait(vj.at[1, :, BLOCK * i : BLOCK * (i + 1)], tsem.at[i])
    multiply(1, False)
    tile = shared(4, bothers)
    rr0, curve0, square = (unpack(tile, i) for i in range(3))
    a0 = rr0 / curve0
    mu = square / curve0
    r1 = r0 - a0 * w1
    u = w1 - mu * r0
    piece = fb[1, zl] - (0.25 * (mu - RIDGE)) * w1
    share(12, x, xmates, pack([u * piece, 0.25 * (r1 * u)]))
    share(16, y, ymates, shared(12, xothers))
    share(20, z, rmates, shared(16, yothers))
    image1 = image(1, w1) - mu * w1
    tile = shared(20, rothers)
    tau = unpack(tile, 1) / unpack(tile, 0)
    for core in (0, 1):

        @pl.when(c == core)
        def _(core=core):
            fin[0, 32 * core : 32 * core + 32] = a0 * r0 + tau * u
            fin[1, 32 * core : 32 * core + 32] = r1 - tau * image1

    copy(fin.at[:, half], fin.at[:, half], esem, sibling)
    wait(fin.at[:, other_half], esem)
    sol[...] = fin[0]
    res[...] = fin[1]
    for made, when in sent:
        if when is None:
            made.wait_send()
        else:
            pl.when(when)(made.wait_send)


def solve(counters, frow, zcol, right):
    vmem = pl.BlockSpec(memory_space=pltpu.VMEM)
    dma = pltpu.SemaphoreType.DMA
    vector, some = (TARGETS, BLOCK), (TARGETS // 2, BLOCK)
    shapes = [
        (2, 4, BLOCK, WIDTH), (3, 2, BLOCK, WIDTH), (BLOCK, WIDTH), (BLOCK, WIDTH), (BLOCK, WIDTH), (8,) + vector, (TARGETS, WIDTH),
        (2, TARGETS // 2, 2 * WIDTH), some, (2, 4) + some, (28, 8, BLOCK), some, (2,) + vector,
    ]
    return pl.pallas_call(
        solve_kernel,
        out_shape=(
            jax.ShapeDtypeStruct(vector, F32),
            jax.ShapeDtypeStruct(vector, F32),
            jax.ShapeDtypeStruct((BLOCK, WIDTH), F32),
        ),
        in_specs=[vmem] * 4,
        out_specs=(vmem,) * 3,
        scratch_shapes=[
            pltpu.VMEM((2 * BLOCK, DEPTH + 128), jnp.bfloat16),
            pltpu.VMEM((2 * BLOCK, WIDTH), F32),
        ]
        + [pltpu.VMEM(shape, F32) for shape in shapes]
        + [
            dma((96,)), dma((8,)), dma((4,)), dma, dma, dma((6,)), dma, dma, dma((8,)), dma((8,)),
            dma((28,)), dma,
        ],
        compiler_params=pltpu.CompilerParams(collective_id=1, has_side_effects=True, vmem_limit_bytes=40 << 20),
        name="solve",
    )(counters.reshape(4 * ROWS, DEPTH), frow, zcol.reshape(4 * ROWS, WIDTH), right)


def on_device(counters, frequencies, phases, targets):
    columns = jnp.concatenate([frequencies.T, jnp.broadcast_to(phases.T, (WIDTH, 128))], axis=1)
    samples, _, rows, zcol, right = gather(counters, targets.T, columns, frequencies, phases)
    solution, residual, gram = solve(samples, rows, zcol, right)
    return solution.T, residual.T, gram


def solution(mesh):
    return jax.shard_map(
        on_device,
        mesh=mesh,
        in_specs=(P("samp", None), P(None, "feat"), P(None, "feat"), P("samp", None)),
        out_specs=(P("samp", None), P("samp", None), P("samp", "feat")),
        check_vma=False,
    )
```

```python
import math

import jax
import jax.numpy as jnp
from jax import lax
from jax.experimental import pallas as pl
from jax.experimental.pallas import tpu as pltpu
from jax.sharding import PartitionSpec as P

RIDGE = 0.05
ROWS, DEPTH, WIDTH, TARGETS, BLOCK = 1024, 512, 512, 64, 128
TOTAL = 32768
STEP = 512
MESH = pl.DeviceIdType.MESH
SINE = (4.442883014678955, -7.308241367340088, 3.6062889099121094, -0.8457635641098022, 0.10920573770999908)
HIGHEST = lax.Precision.HIGHEST
F32 = jnp.float32


def cosine(angle):
    turns = angle * (0.5 / math.pi)
    f = turns - jnp.round(turns)
    square = f * f
    poly = SINE[-1]
    for coefficient in SINE[-2::-1]:
        poly = poly * square + coefficient
    root = poly * f
    return (1.0 - root * root).astype(jnp.bfloat16)


NT = (((1,), (1,)), ((), ()))


def features(block, rows):
    mixed = lax.dot_general(block[:, :DEPTH], rows, NT, preferred_element_type=F32)
    return cosine(mixed + block[:, DEPTH : DEPTH + 1].astype(F32))


def remote(src, dst, send_sem, recv_sem, device):
    return pltpu.make_async_remote_copy(
        src_ref=src, dst_ref=dst, send_sem=send_sem, recv_sem=recv_sem, device_id=device, device_id_type=MESH
    )


def greet(peers):
    barrier = pltpu.get_barrier_semaphore()
    for peer in peers:
        pl.semaphore_signal(barrier, inc=1, device_id=peer, device_id_type=MESH)
    pl.semaphore_wait(barrier, len(peers))


def gather_kernel(cnt, tgt, frq, fcol, phase, cg, tg, fr, zcol, rpart, ssem, rsem, fsend, frecv, lsem):
    s, j = lax.axis_index("samp"), lax.axis_index("feat")
    x, c, zl, zh = lax.rem(s, 4), lax.rem(j, 2), lax.div(j, 2), lax.div(s, 16)
    z = zh * 4 + zl
    right = (s - x + lax.rem(x + 1, 4), j)
    left = (s - x + lax.rem(x + 3, 4), j)
    sibling = (s, j + 1 - 2 * c)

    def along_z(dz, core):
        other = lax.rem(z + dz + 8, 8)
        return (lax.div(other, 4) * 16 + lax.rem(s, 16), lax.rem(other, 4) * 2 + core)

    far = 2 - 4 * c
    greet(
        [right, left, sibling]
        + [along_z(dz, core) for dz in (1, -1) for core in (0, 1)]
        + [along_z(far, 0), along_z(far, 1), along_z(-far, c)]
    )

    half = STEP * c
    a_rows, b_rows = pl.ds(pl.multiple_of(half, 256), 256), pl.ds(pl.multiple_of(half + 256, 256), 256)
    a_cols = pl.ds(pl.multiple_of(half, 256), 256)
    b_cols = pl.ds(pl.multiple_of(half + 256, 256), 256)

    def pair(i, src_c, src_t, slot, part, device):
        rows, cols = (a_rows, a_cols) if part == 0 else (b_rows, b_cols)
        return [
            remote(src_c.at[rows], cg.at[slot, rows], ssem.at[2 * i], rsem.at[2 * i], device),
            remote(src_t.at[:, cols], tg.at[slot, :, cols], ssem.at[2 * i + 1], rsem.at[2 * i + 1], device),
        ]

    def twin(i, slot, part):
        other = STEP - half
        rows = pl.ds(pl.multiple_of(other + 256 * part, 256), 256)
        cols = pl.ds(pl.multiple_of(other + 256 * part, 256), 256)
        return [
            remote(cg.at[slot, rows], cg.at[slot, rows], ssem.at[2 * i], rsem.at[2 * i], sibling),
            remote(tg.at[slot, :, cols], tg.at[slot, :, cols], ssem.at[2 * i + 1], rsem.at[2 * i + 1], sibling),
        ]

    to_right = [pair(0, cnt, tgt, 1, 0, right), pair(1, cnt, tgt, 1, 1, right)]
    to_left = [pair(2, cnt, tgt, 2, 0, left), pair(3, cnt, tgt, 2, 1, left)]
    on_right = pair(4, cg.at[1], tg.at[1], 3, 0, right)
    on_left = pair(5, cg.at[2], tg.at[2], 3, 1, left)
    across = {
        (slot, part): pair(6 + 2 * (slot - 1) + part, cg.at[slot], tg.at[slot], slot, part, sibling)
        for slot in (1, 2, 3)
        for part in (0, 1)
    }

    def go(copies):
        for copy in copies:
            copy.start()

    def got(copies):
        for copy in copies:
            copy.wait_recv()

    go(to_right[0])
    go(to_left[1])
    mine = pl.ds(pl.multiple_of(BLOCK * j, BLOCK), BLOCK)
    spread = []
    for i, (dz, core) in enumerate([(1, 0), (1, 1), (-1, 0), (-1, 1), (far, 0), (far, 1)]):
        spread.append(remote(frq, fr.at[mine], fsend.at[i], frecv.at[2 * (i // 2) + c], along_z(dz, core)))
    spread.append(remote(frq, fr.at[mine], fsend.at[6], frecv.at[6], sibling))
    go(spread)
    go(to_right[1])
    go(to_left[0])
    local = [
        pltpu.make_async_copy(cnt, cg.at[0], lsem.at[0]),
        pltpu.make_async_copy(tgt, tg.at[0], lsem.at[1]),
        pltpu.make_async_copy(frq, fr.at[mine], lsem.at[2]),
    ]
    go(local)
    def columns(slot, rows):
        mixed = jnp.dot(cg[slot, rows, :], fcol[...], preferred_element_type=F32)
        zcol[slot, rows, :] = cosine(mixed + phase[...].astype(F32))
        samples = pl.ds(pl.multiple_of(rows.start, STEP), STEP)
        own = features(frq[...], cg[slot, rows, :])
        rpart[...] += lax.dot_general(tg[slot, :, samples], own, NT, preferred_element_type=F32)

    here, there = pl.ds(pl.multiple_of(half, STEP), STEP), pl.ds(pl.multiple_of(STEP - half, STEP), STEP)
    rpart[...] = jnp.zeros_like(rpart)
    local[0].wait()
    local[1].wait()
    columns(0, here)
    got(to_right[0])
    go(on_right)
    go(across[1, 0])
    got(to_left[1])
    go(on_left)
    go(across[2, 1])
    columns(0, there)
    got(to_right[1])
    go(across[1, 1])
    got(to_left[0])
    go(across[2, 0])
    columns(1, here)
    columns(2, here)
    got(on_right)
    go(across[3, 0])

    def twins(slot):
        for part in (0, 1):
            got(twin(6 + 2 * (slot - 1) + part, slot, part))

    twins(1)
    columns(1, there)
    got(on_left)
    go(across[3, 1])
    twins(2)
    columns(2, there)
    columns(3, here)
    twins(3)
    columns(3, there)
    for i, (dz, core) in enumerate([(-1, 0), (-1, 1), (1, 0), (1, 1), (-2, 0), (2, 1)]):
        source = along_z(dz, core)
        rows = pl.ds(pl.multiple_of(BLOCK * source[1], BLOCK), BLOCK)
        remote(frq, fr.at[rows], fsend.at[i], frecv.at[2 * (i // 2) + core], source).wait_recv()
    rows = pl.ds(pl.multiple_of(BLOCK * sibling[1], BLOCK), BLOCK)
    remote(frq, fr.at[rows], fsend.at[6], frecv.at[6], sibling).wait_recv()
    local[2].wait()
    sent = to_right[0] + to_right[1] + to_left[0] + to_left[1] + on_right + on_left + spread
    for copies in across.values():
        sent = sent + copies
    for copy in sent:
        copy.wait_send()


def gather(counters, targets, frequencies, columns, phases):
    bf16 = jnp.bfloat16
    vmem = pl.BlockSpec(memory_space=pltpu.VMEM)
    return pl.pallas_call(
        gather_kernel,
        out_shape=(
            jax.ShapeDtypeStruct((4, ROWS, DEPTH), bf16),
            jax.ShapeDtypeStruct((4, TARGETS, ROWS), bf16),
            jax.ShapeDtypeStruct((8 * BLOCK, DEPTH + 128), bf16),
            jax.ShapeDtypeStruct((4, ROWS, WIDTH), bf16),
            jax.ShapeDtypeStruct((TARGETS, BLOCK), F32),
        ),
        in_specs=[vmem] * 5,
        out_specs=(vmem,) * 5,
        scratch_shapes=[
            pltpu.SemaphoreType.DMA((24,)),
            pltpu.SemaphoreType.DMA((24,)),
            pltpu.SemaphoreType.DMA((7,)),
            pltpu.SemaphoreType.DMA((7,)),
            pltpu.SemaphoreType.DMA((3,)),
        ],
        compiler_params=pltpu.CompilerParams(collective_id=0, has_side_effects=True, vmem_limit_bytes=32 << 20),
        name="gather",
    )(counters, targets, frequencies, columns, phases)


def solve_kernel(
    cnt, frow, zcol, right, sol, res, gram,
    pair, acc, part, ybuf, zsend, zrecv, gother, rh, rj, vj, first, fb, sums, w1buf, fin,
    ssem, hsem, rsem, osem, psem, ysem, zsem, gsem, fsem, tsem, xsem, esem,
):
    s, j = lax.axis_index("samp"), lax.axis_index("feat")
    x, b = lax.rem(s, 4), lax.div(s, 4)
    y, zh = lax.rem(b, 4), lax.div(b, 4)
    c, zl = lax.rem(j, 2), lax.div(j, 2)
    diag = b == j
    sibling = (s, j + 1 - 2 * c)
    xothers = [lax.rem(x + d, 4) for d in (1, 2, 3)]
    xmates = [(b * 4 + o, j) for o in xothers]
    bothers = [lax.rem(b + e, 8) for e in range(1, 8)]
    bmates = [(o * 4 + x, j) for o in bothers]
    fothers = [lax.rem(j + e, 8) for e in range(1, 8)]
    fmates = [(s, o) for o in fothers]
    zothers = [lax.rem(zl + d, 4) for d in (1, 2, 3)]
    zmates = [(s, o * 2 + c) for o in zothers]
    yothers = [lax.rem(y + d, 4) for d in (1, 2, 3)]
    ymates = [((zh * 4 + o) * 4 + x, j) for o in yothers]
    z = zh * 4 + zl
    rothers = [lax.rem(z + e, 8) for e in range(1, 8)]
    rmates = [((lax.div(o, 4) * 4 + y) * 4 + x, lax.rem(o, 4) * 2 + c) for o in rothers]
    across = [((1 - zh) * 16 + y * 4 + x, o * 2 + c) for o in zothers]
    down = lax.div(b, 2)
    same = lax.div(zl, 2) == zh
    near = jnp.where(same, zl == down, zl == 3 * (1 - zh))
    to_zh = jnp.where(same, zh, 1 - zh)
    skip = jnp.where(near, 2, 0)
    spread_to = [((to_zh * 4 + lax.rem(y + skip + d, 4)) * 4 + o, down * 2 + c) for d in (0, 1) for o in range(4)]
    spread_from = []
    for h in (0, 1):
        source_y, source_zh = lax.rem(zl, 2) * 2 + h, lax.div(zl, 2)
        far = jnp.where(lax.rem(y + 4 - source_y, 4) < 2, 1, 0)
        inside = zl + far * (1 - 2 * lax.rem(zl, 2))
        outside = jnp.where(source_zh == 0, 3 - far, far)
        source_zl = jnp.where(zh == source_zh, inside, outside)
        spread_from += [((zl * 2 + h) * 4 + o, source_zl * 2 + c) for o in range(4)]

    barrier = pltpu.get_barrier_semaphore()
    peers = xmates + bmates + fmates + across + spread_from
    for peer in peers:
        pl.semaphore_signal(barrier, inc=1, device_id=peer, device_id_type=MESH)

    count = [0]
    sent = []

    def copy(src, dst, recv_sem, device, when=None):
        made = remote(src, dst, ssem.at[count[0]], recv_sem, device)
        count[0] += 1
        sent.append((made, when))
        if when is None:
            made.start()
        else:
            pl.when(when)(made.start)

    def wait(ref, sem):
        remote(ref, ref, ssem.at[0], sem, sibling).wait_recv()

    def lanes(block, size=BLOCK):
        return pl.ds(pl.multiple_of(block * size, size), size)

    half, other_half = pl.ds(32 * c, 32), pl.ds(32 * (1 - c), 32)

    def two_blocks(which, slot, first_d):
        steps = (first_d, first_d + 1)
        for n, d in enumerate(steps):
            row = pl.multiple_of((which * 4 + lax.rem(y + d, 4)) * BLOCK, BLOCK)
            pair[n * BLOCK : (n + 1) * BLOCK, :] = frow[pl.ds(row, BLOCK), :]
        acc[...] = jnp.zeros_like(acc)

        @pl.loop(0, 4 * ROWS // STEP)
        def _(i):
            chunk = pl.ds(pl.multiple_of(i * STEP, STEP), STEP)
            acc[...] += jnp.dot(features(pair[...], cnt[chunk, :]), zcol[chunk, :], preferred_element_type=F32)

        if (slot, first_d) == (0, 1):
            pl.semaphore_wait(barrier, len(peers))
            for peer in bmates:
                copy(right, rh.at[b], hsem.at[b], peer)
        for n, d in enumerate(steps):
            part[slot, d - 1] = acc[n * BLOCK : (n + 1) * BLOCK, :]
            if d < 4:
                copy(part.at[slot, d - 1], ybuf.at[d - 1, slot], ysem.at[3 * slot + d - 1], ymates[d - 1])

    two_blocks(1 - zh, 0, 1)
    two_blocks(1 - zh, 0, 3)
    two_blocks(zh, 1, 1)
    rh[b] = right[...]
    for o in bothers:
        wait(rh.at[o], hsem.at[o])
    total = rh[0]
    for o in range(1, 8):
        total = total + rh[o]
    total = total * (1.0 / math.sqrt(TOTAL))
    rj[:, lanes(x)] = total
    for peer in xmates:
        copy(rj.at[:, lanes(x)], rj.at[:, lanes(x)], rsem.at[x], peer)
    for core in (0, 1):

        @pl.when(jnp.logical_and(diag, c == core))
        def _(core=core):
            first[...] = total[32 * core : 32 * core + 32]

    for o, peer in zip(fothers, fmates):
        copy(rj.at[pl.ds(32 * lax.rem(o, 2), 32), lanes(x)], first, psem, peer, diag)

    def over_y(slot):
        total = part[slot, 3]
        for d in range(3):
            wait(ybuf.at[d, slot], ysem.at[3 * slot + d])
            total = total + ybuf[d, slot]
        return total

    zsend[...] = over_y(0)
    copy(zsend, zrecv, zsem, (((1 - zh) * 4 + y) * 4 + x, j))
    two_blocks(zh, 1, 3)
    for o in xothers:
        wait(rj.at[:, lanes(o)], rsem.at[o])
    for core in (0, 1):

        @pl.when(c == core)
        def _(core=core):
            vj[0, :, core * WIDTH : (core + 1) * WIDTH] = rj[32 * core : 32 * core + 32, :]

    copy(rj.at[other_half, :], vj.at[0, :, lanes(c, WIDTH)], osem, sibling)
    gram[...] = over_y(1)
    wait(vj.at[0, :, lanes(1 - c, WIDTH)], osem)

    @pl.when(jnp.logical_not(diag))
    def _():
        wait(first, psem)

    wait(zrecv, zsem)
    gram[...] = (gram[...] + zrecv[...]) * (1.0 / TOTAL)
    copy(gram, gother, gsem, sibling)

    def multiply(it, wait_gram):
        own = lax.dot_general(vj[it, :, lanes(c, WIDTH)], gram[...], NT, precision=HIGHEST, preferred_element_type=F32)
        if wait_gram:
            wait(gother, gsem)
        fb[it, zl] = own + lax.dot_general(
            vj[it, :, lanes(1 - c, WIDTH)], gother[...], NT, precision=HIGHEST, preferred_element_type=F32
        )
        for peer in zmates:
            copy(fb.at[it, zl], fb.at[it, zl], fsem.at[4 * it + zl], peer)

    def image(it, vector):
        for o in zothers:
            wait(fb.at[it, o], fsem.at[4 * it + o])
        return ((fb[it, 0] + fb[it, 1]) + (fb[it, 2] + fb[it, 3])) + RIDGE * vector

    some = (TARGETS // 2, BLOCK)
    match = lax.broadcasted_iota(jnp.int32, some, 0) == lax.broadcasted_iota(jnp.int32, some, 1)
    sublane = lax.broadcasted_iota(jnp.int32, (8, BLOCK), 0)

    def pack(values):
        tile = jnp.zeros((8, BLOCK), F32)
        for i, value in enumerate(values):
            sums = jnp.where(match, jnp.sum(value, axis=1, keepdims=True), 0.0)
            tile = jnp.where(sublane == i, jnp.sum(sums, axis=0, keepdims=True), tile)
        return tile

    def unpack(tile, i):
        return jnp.sum(jnp.where(match, tile[i : i + 1], 0.0), axis=1, keepdims=True)

    def share(base, mine, mates, tile):
        sums[base + mine] = tile
        for peer in mates:
            copy(sums.at[base + mine], sums.at[base + mine], xsem.at[base + mine], peer)

    def shared(base, others):
        for o in others:
            wait(sums.at[base + o], xsem.at[base + o])
        total = sums[base]
        for i in range(1, len(others) + 1):
            total = total + sums[base + i]
        return total

    multiply(0, True)
    r0 = first[...]
    w1 = image(0, r0)
    w1buf[...] = w1
    place = lax.rem(b, 2) * 4 + x
    for peer in spread_to:
        copy(w1buf, vj.at[1, :, lanes(place)], tsem.at[place], peer)
    share(0, x, xmates, pack([r0 * r0, r0 * w1, w1 * w1]))
    share(4, b, bmates, shared(0, xothers))
    for i in range(8):
        wait(vj.at[1, :, BLOCK * i : BLOCK * (i + 1)], tsem.at[i])
    multiply(1, False)
    tile = shared(4, bothers)
    rr0, curve0, square = (unpack(tile, i) for i in range(3))
    a0 = rr0 / curve0
    mu = square / curve0
    r1 = r0 - a0 * w1
    u = w1 - mu * r0
    piece = fb[1, zl] - (0.25 * (mu - RIDGE)) * w1
    share(12, x, xmates, pack([u * piece, 0.25 * (r1 * u)]))
    share(16, y, ymates, shared(12, xothers))
    share(20, z, rmates, shared(16, yothers))
    image1 = image(1, w1) - mu * w1
    tile = shared(20, rothers)
    tau = unpack(tile, 1) / unpack(tile, 0)
    for core in (0, 1):

        @pl.when(c == core)
        def _(core=core):
            fin[0, 32 * core : 32 * core + 32] = a0 * r0 + tau * u
            fin[1, 32 * core : 32 * core + 32] = r1 - tau * image1

    copy(fin.at[:, half], fin.at[:, half], esem, sibling)
    wait(fin.at[:, other_half], esem)
    sol[...] = fin[0]
    res[...] = fin[1]
    for made, when in sent:
        if when is None:
            made.wait_send()
        else:
            pl.when(when)(made.wait_send)


def solve(counters, frow, zcol, right):
    vmem = pl.BlockSpec(memory_space=pltpu.VMEM)
    dma = pltpu.SemaphoreType.DMA
    vector, some = (TARGETS, BLOCK), (TARGETS // 2, BLOCK)
    shapes = [
        (2, 4, BLOCK, WIDTH), (3, 2, BLOCK, WIDTH), (BLOCK, WIDTH), (BLOCK, WIDTH), (BLOCK, WIDTH), (8,) + vector, (TARGETS, WIDTH),
        (2, TARGETS // 2, 2 * WIDTH), some, (2, 4) + some, (28, 8, BLOCK), some, (2,) + vector,
    ]
    return pl.pallas_call(
        solve_kernel,
        out_shape=(
            jax.ShapeDtypeStruct(vector, F32),
            jax.ShapeDtypeStruct(vector, F32),
            jax.ShapeDtypeStruct((BLOCK, WIDTH), F32),
        ),
        in_specs=[vmem] * 4,
        out_specs=(vmem,) * 3,
        scratch_shapes=[
            pltpu.VMEM((2 * BLOCK, DEPTH + 128), jnp.bfloat16),
            pltpu.VMEM((2 * BLOCK, WIDTH), F32),
        ]
        + [pltpu.VMEM(shape, F32) for shape in shapes]
        + [
            dma((96,)), dma((8,)), dma((4,)), dma, dma, dma((6,)), dma, dma, dma((8,)), dma((8,)),
            dma((28,)), dma,
        ],
        compiler_params=pltpu.CompilerParams(collective_id=1, has_side_effects=True, vmem_limit_bytes=40 << 20),
        name="solve",
    )(counters.reshape(4 * ROWS, DEPTH), frow, zcol.reshape(4 * ROWS, WIDTH), right)


def on_device(counters, frequencies, phases, targets):
    first = lax.rem(lax.axis_index("samp"), 4) * BLOCK
    quarter = lax.dynamic_slice_in_dim(frequencies, first, BLOCK, 1).T
    shift = lax.dynamic_slice_in_dim(phases, first, BLOCK, 1).T
    columns = jnp.concatenate([quarter, jnp.broadcast_to(shift, (BLOCK, 128))], axis=1)
    samples, _, rows, zcol, right = gather(counters, targets.T, columns, frequencies, phases)
    solution, residual, gram = solve(samples, rows, zcol, right)
    return solution.T, residual.T, gram


def solution(mesh):
    return jax.shard_map(
        on_device,
        mesh=mesh,
        in_specs=(P("samp", None), P(None, "feat"), P(None, "feat"), P("samp", None)),
        out_specs=(P("samp", None), P("samp", None), P("samp", "feat")),
        check_vma=False,
    )
```

```python
import math

import jax
import jax.numpy as jnp
from jax import lax
from jax.experimental import pallas as pl
from jax.experimental.pallas import tpu as pltpu
from jax.sharding import PartitionSpec as P

RIDGE = 0.05
ROWS, DEPTH, WIDTH, TARGETS, BLOCK = 1024, 512, 512, 64, 128
TOTAL = 32768
STEP = 512
MESH = pl.DeviceIdType.MESH
SINE = (4.442883014678955, -7.308241367340088, 3.6062889099121094, -0.8457635641098022, 0.10920573770999908)
HIGHEST = lax.Precision.HIGHEST
F32 = jnp.float32


def cosine(angle):
    turns = angle * (0.5 / math.pi)
    f = turns - jnp.round(turns)
    square = f * f
    poly = SINE[-1]
    for coefficient in SINE[-2::-1]:
        poly = poly * square + coefficient
    root = poly * f
    return (1.0 - root * root).astype(jnp.bfloat16)


NT = (((1,), (1,)), ((), ()))


def features(block, rows):
    mixed = lax.dot_general(block[:, :DEPTH], rows, NT, preferred_element_type=F32)
    return cosine(mixed + block[:, DEPTH : DEPTH + 1].astype(F32))


def remote(src, dst, send_sem, recv_sem, device):
    return pltpu.make_async_remote_copy(
        src_ref=src, dst_ref=dst, send_sem=send_sem, recv_sem=recv_sem, device_id=device, device_id_type=MESH
    )


def greet(peers):
    barrier = pltpu.get_barrier_semaphore()
    for peer in peers:
        pl.semaphore_signal(barrier, inc=1, device_id=peer, device_id_type=MESH)
    pl.semaphore_wait(barrier, len(peers))


def gather_kernel(cnt, tgt, frq, fcol, phase, cg, fr, zcol, rpart, tg, ssem, rsem, fsend, frecv, lsem):
    s, j = lax.axis_index("samp"), lax.axis_index("feat")
    x, c, zl, zh = lax.rem(s, 4), lax.rem(j, 2), lax.div(j, 2), lax.div(s, 16)
    z = zh * 4 + zl
    right = (s - x + lax.rem(x + 1, 4), j)
    left = (s - x + lax.rem(x + 3, 4), j)
    sibling = (s, j + 1 - 2 * c)

    def along_z(dz, core):
        other = lax.rem(z + dz + 8, 8)
        return (lax.div(other, 4) * 16 + lax.rem(s, 16), lax.rem(other, 4) * 2 + core)

    far = 2 - 4 * c
    greet(
        [right, left, sibling]
        + [along_z(dz, core) for dz in (1, -1) for core in (0, 1)]
        + [along_z(far, 0), along_z(far, 1), along_z(-far, c)]
    )

    half = STEP * c
    a_rows, b_rows = pl.ds(pl.multiple_of(half, 256), 256), pl.ds(pl.multiple_of(half + 256, 256), 256)
    a_cols = pl.ds(pl.multiple_of(half, 256), 256)
    b_cols = pl.ds(pl.multiple_of(half + 256, 256), 256)

    def pair(i, src_c, src_t, slot, part, device):
        rows, cols = (a_rows, a_cols) if part == 0 else (b_rows, b_cols)
        return [
            remote(src_c.at[rows], cg.at[slot, rows], ssem.at[2 * i], rsem.at[2 * i], device),
            remote(src_t.at[:, cols], tg.at[slot, :, cols], ssem.at[2 * i + 1], rsem.at[2 * i + 1], device),
        ]

    def twin(i, slot, part):
        other = STEP - half
        rows = pl.ds(pl.multiple_of(other + 256 * part, 256), 256)
        cols = pl.ds(pl.multiple_of(other + 256 * part, 256), 256)
        return [
            remote(cg.at[slot, rows], cg.at[slot, rows], ssem.at[2 * i], rsem.at[2 * i], sibling),
            remote(tg.at[slot, :, cols], tg.at[slot, :, cols], ssem.at[2 * i + 1], rsem.at[2 * i + 1], sibling),
        ]

    to_right = [pair(0, cnt, tgt, 1, 0, right), pair(1, cnt, tgt, 1, 1, right)]
    to_left = [pair(2, cnt, tgt, 2, 0, left), pair(3, cnt, tgt, 2, 1, left)]
    on_right = pair(4, cg.at[1], tg.at[1], 3, 0, right)
    on_left = pair(5, cg.at[2], tg.at[2], 3, 1, left)
    across = {
        (slot, part): pair(6 + 2 * (slot - 1) + part, cg.at[slot], tg.at[slot], slot, part, sibling)
        for slot in (1, 2, 3)
        for part in (0, 1)
    }

    def go(copies):
        for copy in copies:
            copy.start()

    def got(copies):
        for copy in copies:
            copy.wait_recv()

    go(to_right[0])
    go(to_left[1])
    quarter = pl.ds(pl.multiple_of(BLOCK * x, BLOCK), BLOCK)
    mine = pl.ds(pl.multiple_of(BLOCK * j, BLOCK), BLOCK)
    spread = []
    for i, (dz, core) in enumerate([(1, 0), (1, 1), (-1, 0), (-1, 1), (far, 0), (far, 1)]):
        spread.append(remote(frq.at[quarter], fr.at[mine], fsend.at[i], frecv.at[2 * (i // 2) + c], along_z(dz, core)))
    spread.append(remote(frq.at[quarter], fr.at[mine], fsend.at[6], frecv.at[6], sibling))
    go(spread)
    go(to_right[1])
    go(to_left[0])
    local = [
        pltpu.make_async_copy(cnt, cg.at[0], lsem.at[0]),
        pltpu.make_async_copy(tgt, tg.at[0], lsem.at[1]),
        pltpu.make_async_copy(frq.at[quarter], fr.at[mine], lsem.at[2]),
    ]
    go(local)
    def columns(slot, rows):
        mixed = jnp.dot(cg[slot, rows, :], fcol[...], preferred_element_type=F32)
        zcol[slot, rows, :] = cosine(mixed + phase[...].astype(F32))
        samples = pl.ds(pl.multiple_of(rows.start, STEP), STEP)
        own = features(frq[quarter, :], cg[slot, rows, :])
        rpart[...] += lax.dot_general(tg[slot, :, samples], own, NT, preferred_element_type=F32)

    here, there = pl.ds(pl.multiple_of(half, STEP), STEP), pl.ds(pl.multiple_of(STEP - half, STEP), STEP)
    rpart[...] = jnp.zeros_like(rpart)
    local[0].wait()
    local[1].wait()
    columns(0, here)
    got(to_right[0])
    go(on_right)
    go(across[1, 0])
    got(to_left[1])
    go(on_left)
    go(across[2, 1])
    columns(0, there)
    got(to_right[1])
    go(across[1, 1])
    got(to_left[0])
    go(across[2, 0])
    columns(1, here)
    columns(2, here)
    got(on_right)
    go(across[3, 0])

    def twins(slot):
        for part in (0, 1):
            got(twin(6 + 2 * (slot - 1) + part, slot, part))

    twins(1)
    columns(1, there)
    got(on_left)
    go(across[3, 1])
    twins(2)
    columns(2, there)
    columns(3, here)
    twins(3)
    columns(3, there)
    for i, (dz, core) in enumerate([(-1, 0), (-1, 1), (1, 0), (1, 1), (-2, 0), (2, 1)]):
        source = along_z(dz, core)
        rows = pl.ds(pl.multiple_of(BLOCK * source[1], BLOCK), BLOCK)
        remote(frq.at[quarter], fr.at[rows], fsend.at[i], frecv.at[2 * (i // 2) + core], source).wait_recv()
    rows = pl.ds(pl.multiple_of(BLOCK * sibling[1], BLOCK), BLOCK)
    remote(frq.at[quarter], fr.at[rows], fsend.at[6], frecv.at[6], sibling).wait_recv()
    local[2].wait()
    sent = to_right[0] + to_right[1] + to_left[0] + to_left[1] + on_right + on_left + spread
    for copies in across.values():
        sent = sent + copies
    for copy in sent:
        copy.wait_send()


def gather(counters, targets, frequencies, columns, phases):
    bf16 = jnp.bfloat16
    vmem = pl.BlockSpec(memory_space=pltpu.VMEM)
    return pl.pallas_call(
        gather_kernel,
        out_shape=(
            jax.ShapeDtypeStruct((4, ROWS, DEPTH), bf16),
            jax.ShapeDtypeStruct((8 * BLOCK, DEPTH + 128), bf16),
            jax.ShapeDtypeStruct((4, ROWS, WIDTH), bf16),
            jax.ShapeDtypeStruct((TARGETS, BLOCK), F32),
        ),
        in_specs=[vmem] * 5,
        out_specs=(vmem,) * 4,
        scratch_shapes=[
            pltpu.VMEM((4, TARGETS, ROWS), bf16),
            pltpu.SemaphoreType.DMA((24,)),
            pltpu.SemaphoreType.DMA((24,)),
            pltpu.SemaphoreType.DMA((7,)),
            pltpu.SemaphoreType.DMA((7,)),
            pltpu.SemaphoreType.DMA((3,)),
        ],
        compiler_params=pltpu.CompilerParams(collective_id=0, has_side_effects=True, vmem_limit_bytes=32 << 20),
        name="gather",
    )(counters, targets, frequencies, columns, phases)


def solve_kernel(
    cnt, frow, zcol, right, sol, res, gram,
    pair, acc, part, ybuf, zsend, zrecv, gother, rh, rj, vj, first, fb, sums, w1buf, fin,
    ssem, hsem, rsem, osem, psem, ysem, zsem, gsem, fsem, tsem, xsem, esem,
):
    s, j = lax.axis_index("samp"), lax.axis_index("feat")
    x, b = lax.rem(s, 4), lax.div(s, 4)
    y, zh = lax.rem(b, 4), lax.div(b, 4)
    c, zl = lax.rem(j, 2), lax.div(j, 2)
    diag = b == j
    sibling = (s, j + 1 - 2 * c)
    xothers = [lax.rem(x + d, 4) for d in (1, 2, 3)]
    xmates = [(b * 4 + o, j) for o in xothers]
    bothers = [lax.rem(b + e, 8) for e in range(1, 8)]
    bmates = [(o * 4 + x, j) for o in bothers]
    fothers = [lax.rem(j + e, 8) for e in range(1, 8)]
    fmates = [(s, o) for o in fothers]
    zothers = [lax.rem(zl + d, 4) for d in (1, 2, 3)]
    zmates = [(s, o * 2 + c) for o in zothers]
    yothers = [lax.rem(y + d, 4) for d in (1, 2, 3)]
    ymates = [((zh * 4 + o) * 4 + x, j) for o in yothers]
    z = zh * 4 + zl
    rothers = [lax.rem(z + e, 8) for e in range(1, 8)]
    rmates = [((lax.div(o, 4) * 4 + y) * 4 + x, lax.rem(o, 4) * 2 + c) for o in rothers]
    across = [((1 - zh) * 16 + y * 4 + x, o * 2 + c) for o in zothers]
    down = lax.div(b, 2)
    same = lax.div(zl, 2) == zh
    near = jnp.where(same, zl == down, zl == 3 * (1 - zh))
    to_zh = jnp.where(same, zh, 1 - zh)
    skip = jnp.where(near, 2, 0)
    spread_to = [((to_zh * 4 + lax.rem(y + skip + d, 4)) * 4 + o, down * 2 + c) for d in (0, 1) for o in range(4)]
    spread_from = []
    for h in (0, 1):
        source_y, source_zh = lax.rem(zl, 2) * 2 + h, lax.div(zl, 2)
        far = jnp.where(lax.rem(y + 4 - source_y, 4) < 2, 1, 0)
        inside = zl + far * (1 - 2 * lax.rem(zl, 2))
        outside = jnp.where(source_zh == 0, 3 - far, far)
        source_zl = jnp.where(zh == source_zh, inside, outside)
        spread_from += [((zl * 2 + h) * 4 + o, source_zl * 2 + c) for o in range(4)]

    barrier = pltpu.get_barrier_semaphore()
    peers = xmates + bmates + fmates + across + spread_from
    for peer in peers:
        pl.semaphore_signal(barrier, inc=1, device_id=peer, device_id_type=MESH)

    count = [0]
    sent = []

    def copy(src, dst, recv_sem, device, when=None):
        made = remote(src, dst, ssem.at[count[0]], recv_sem, device)
        count[0] += 1
        sent.append((made, when))
        if when is None:
            made.start()
        else:
            pl.when(when)(made.start)

    def wait(ref, sem):
        remote(ref, ref, ssem.at[0], sem, sibling).wait_recv()

    def lanes(block, size=BLOCK):
        return pl.ds(pl.multiple_of(block * size, size), size)

    half, other_half = pl.ds(32 * c, 32), pl.ds(32 * (1 - c), 32)

    def two_blocks(which, slot, first_d):
        steps = (first_d, first_d + 1)
        for n, d in enumerate(steps):
            row = pl.multiple_of((which * 4 + lax.rem(y + d, 4)) * BLOCK, BLOCK)
            pair[n * BLOCK : (n + 1) * BLOCK, :] = frow[pl.ds(row, BLOCK), :]
        acc[...] = jnp.zeros_like(acc)

        @pl.loop(0, 4 * ROWS // STEP)
        def _(i):
            chunk = pl.ds(pl.multiple_of(i * STEP, STEP), STEP)
            acc[...] += jnp.dot(features(pair[...], cnt[chunk, :]), zcol[chunk, :], preferred_element_type=F32)

        if (slot, first_d) == (0, 1):
            pl.semaphore_wait(barrier, len(peers))
            for peer in bmates:
                copy(right, rh.at[b], hsem.at[b], peer)
        for n, d in enumerate(steps):
            part[slot, d - 1] = acc[n * BLOCK : (n + 1) * BLOCK, :]
            if d < 4:
                copy(part.at[slot, d - 1], ybuf.at[d - 1, slot], ysem.at[3 * slot + d - 1], ymates[d - 1])

    two_blocks(1 - zh, 0, 1)
    two_blocks(1 - zh, 0, 3)
    two_blocks(zh, 1, 1)
    rh[b] = right[...]
    for o in bothers:
        wait(rh.at[o], hsem.at[o])
    total = rh[0]
    for o in range(1, 8):
        total = total + rh[o]
    total = total * (1.0 / math.sqrt(TOTAL))
    rj[:, lanes(x)] = total
    for peer in xmates:
        copy(rj.at[:, lanes(x)], rj.at[:, lanes(x)], rsem.at[x], peer)
    for core in (0, 1):

        @pl.when(jnp.logical_and(diag, c == core))
        def _(core=core):
            first[...] = total[32 * core : 32 * core + 32]

    for o, peer in zip(fothers, fmates):
        copy(rj.at[pl.ds(32 * lax.rem(o, 2), 32), lanes(x)], first, psem, peer, diag)

    def over_y(slot):
        total = part[slot, 3]
        for d in range(3):
            wait(ybuf.at[d, slot], ysem.at[3 * slot + d])
            total = total + ybuf[d, slot]
        return total

    zsend[...] = over_y(0)
    copy(zsend, zrecv, zsem, (((1 - zh) * 4 + y) * 4 + x, j))
    two_blocks(zh, 1, 3)
    for o in xothers:
        wait(rj.at[:, lanes(o)], rsem.at[o])
    for core in (0, 1):

        @pl.when(c == core)
        def _(core=core):
            vj[0, :, core * WIDTH : (core + 1) * WIDTH] = rj[32 * core : 32 * core + 32, :]

    copy(rj.at[other_half, :], vj.at[0, :, lanes(c, WIDTH)], osem, sibling)
    gram[...] = over_y(1)
    wait(vj.at[0, :, lanes(1 - c, WIDTH)], osem)

    @pl.when(jnp.logical_not(diag))
    def _():
        wait(first, psem)

    wait(zrecv, zsem)
    gram[...] = (gram[...] + zrecv[...]) * (1.0 / TOTAL)
    copy(gram, gother, gsem, sibling)

    def multiply(it, wait_gram):
        own = lax.dot_general(vj[it, :, lanes(c, WIDTH)], gram[...], NT, precision=HIGHEST, preferred_element_type=F32)
        if wait_gram:
            wait(gother, gsem)
        fb[it, zl] = own + lax.dot_general(
            vj[it, :, lanes(1 - c, WIDTH)], gother[...], NT, precision=HIGHEST, preferred_element_type=F32
        )
        for peer in zmates:
            copy(fb.at[it, zl], fb.at[it, zl], fsem.at[4 * it + zl], peer)

    def image(it, vector):
        for o in zothers:
            wait(fb.at[it, o], fsem.at[4 * it + o])
        return ((fb[it, 0] + fb[it, 1]) + (fb[it, 2] + fb[it, 3])) + RIDGE * vector

    some = (TARGETS // 2, BLOCK)
    match = lax.broadcasted_iota(jnp.int32, some, 0) == lax.broadcasted_iota(jnp.int32, some, 1)
    sublane = lax.broadcasted_iota(jnp.int32, (8, BLOCK), 0)

    def pack(values):
        tile = jnp.zeros((8, BLOCK), F32)
        for i, value in enumerate(values):
            sums = jnp.where(match, jnp.sum(value, axis=1, keepdims=True), 0.0)
            tile = jnp.where(sublane == i, jnp.sum(sums, axis=0, keepdims=True), tile)
        return tile

    def unpack(tile, i):
        return jnp.sum(jnp.where(match, tile[i : i + 1], 0.0), axis=1, keepdims=True)

    def share(base, mine, mates, tile):
        sums[base + mine] = tile
        for peer in mates:
            copy(sums.at[base + mine], sums.at[base + mine], xsem.at[base + mine], peer)

    def shared(base, others):
        for o in others:
            wait(sums.at[base + o], xsem.at[base + o])
        total = sums[base]
        for i in range(1, len(others) + 1):
            total = total + sums[base + i]
        return total

    multiply(0, True)
    r0 = first[...]
    w1 = image(0, r0)
    w1buf[...] = w1
    place = lax.rem(b, 2) * 4 + x
    for peer in spread_to:
        copy(w1buf, vj.at[1, :, lanes(place)], tsem.at[place], peer)
    share(0, x, xmates, pack([r0 * r0, r0 * w1, w1 * w1]))
    share(4, b, bmates, shared(0, xothers))
    for i in range(8):
        wait(vj.at[1, :, BLOCK * i : BLOCK * (i + 1)], tsem.at[i])
    multiply(1, False)
    tile = shared(4, bothers)
    rr0, curve0, square = (unpack(tile, i) for i in range(3))
    a0 = rr0 / curve0
    mu = square / curve0
    r1 = r0 - a0 * w1
    u = w1 - mu * r0
    piece = fb[1, zl] - (0.25 * (mu - RIDGE)) * w1
    share(12, x, xmates, pack([u * piece, 0.25 * (r1 * u)]))
    share(16, y, ymates, shared(12, xothers))
    share(20, z, rmates, shared(16, yothers))
    image1 = image(1, w1) - mu * w1
    tile = shared(20, rothers)
    tau = unpack(tile, 1) / unpack(tile, 0)
    for core in (0, 1):

        @pl.when(c == core)
        def _(core=core):
            fin[0, 32 * core : 32 * core + 32] = a0 * r0 + tau * u
            fin[1, 32 * core : 32 * core + 32] = r1 - tau * image1

    copy(fin.at[:, half], fin.at[:, half], esem, sibling)
    wait(fin.at[:, other_half], esem)
    sol[...] = fin[0]
    res[...] = fin[1]
    for made, when in sent:
        if when is None:
            made.wait_send()
        else:
            pl.when(when)(made.wait_send)


def solve(counters, frow, zcol, right):
    vmem = pl.BlockSpec(memory_space=pltpu.VMEM)
    dma = pltpu.SemaphoreType.DMA
    vector, some = (TARGETS, BLOCK), (TARGETS // 2, BLOCK)
    shapes = [
        (2, 4, BLOCK, WIDTH), (3, 2, BLOCK, WIDTH), (BLOCK, WIDTH), (BLOCK, WIDTH), (BLOCK, WIDTH), (8,) + vector, (TARGETS, WIDTH),
        (2, TARGETS // 2, 2 * WIDTH), some, (2, 4) + some, (28, 8, BLOCK), some, (2,) + vector,
    ]
    return pl.pallas_call(
        solve_kernel,
        out_shape=(
            jax.ShapeDtypeStruct(vector, F32),
            jax.ShapeDtypeStruct(vector, F32),
            jax.ShapeDtypeStruct((BLOCK, WIDTH), F32),
        ),
        in_specs=[vmem] * 4,
        out_specs=(vmem,) * 3,
        scratch_shapes=[
            pltpu.VMEM((2 * BLOCK, DEPTH + 128), jnp.bfloat16),
            pltpu.VMEM((2 * BLOCK, WIDTH), F32),
        ]
        + [pltpu.VMEM(shape, F32) for shape in shapes]
        + [
            dma((96,)), dma((8,)), dma((4,)), dma, dma, dma((6,)), dma, dma, dma((8,)), dma((8,)),
            dma((28,)), dma,
        ],
        compiler_params=pltpu.CompilerParams(collective_id=1, has_side_effects=True, vmem_limit_bytes=40 << 20),
        name="solve",
    )(counters.reshape(4 * ROWS, DEPTH), frow, zcol.reshape(4 * ROWS, WIDTH), right)


def on_device(counters, frequencies, phases, targets):
    columns = jnp.concatenate([frequencies.T, jnp.broadcast_to(phases.T, (WIDTH, 128))], axis=1)
    samples, rows, zcol, right = gather(counters, targets.T, columns, frequencies, phases)
    solution, residual, gram = solve(samples, rows, zcol, right)
    return solution.T, residual.T, gram


def solution(mesh):
    return jax.shard_map(
        on_device,
        mesh=mesh,
        in_specs=(P("samp", None), P(None, "feat"), P(None, "feat"), P("samp", None)),
        out_specs=(P("samp", None), P("samp", None), P("samp", "feat")),
        check_vma=False,
    )
```
